32 devices in a mesh: gx: 4 (over x, core), gy: 8 (over z, y).
Axes of the slice: x: 2, y: 2, z: 4, core: 2. Of those that a mesh axis runs over, the one named last changes fastest.
Arguments:
- samples: bfloat16 [64, 128, 32, 256], P('gx', 'gy'), may hold values from -6 to 6
- leaf_basis: bfloat16 [64, 256], replicated, may hold values from -0.375 to 0.375
- transfer: bfloat16 [5, 64, 256], replicated, may hold values from -0.5 to 0.5
- coupling: bfloat16 [5, 7, 64, 448], replicated, may hold values from -0.15625 to 0.15625
- near_tiles: bfloat16 [9, 256, 256], replicated, may hold values from -0.125 to 0.125
- codes_local: int32 [64, 128, 4, 27], P('gx', 'gy'), may hold values from 0 to 35, as said below
- counts_local: int32 [64, 128, 4], P('gx', 'gy'), may hold values from 1 to 27, as said below
- codes_upper: int32 [40, 27], replicated, may hold values from 0 to 35, as said below
- counts_upper: int32 [40], replicated, may hold values from 1 to 27, as said below
Outputs:
- response: bfloat16 [64, 128, 32, 256], P('gx', 'gy')
The draws below stay inside these ranges and needn't reach their ends.
Inputs may be any that keep to these rules, and one draw needn't show every extreme that they name: `codes_local`: entries [i, j, l, :] with i and j multiples of 2^l hold the list of the level-l cluster whose first leaf is (i, j); other entries are not read. Its first count entries are distinct codes a * 6 + b of clusters more than one step away from the target in some direction. `counts_local`: length of the list stored at the same position. `codes_upper`: row n is the list of the n-th cluster of level 4 and coarser, levels in order from 4, row-major within a level, each level with half the rows and columns of the one before and the last with 2 rows; first count entries distinct codes of clusters more than one step away from the target in some direction. `counts_upper`: length of the list of the same row.
All inputs are finite; a program needn't handle non-finite values.
Results may differ from the reference program's by a relative error of at most 0.0095.
Values may be sent and summed in bfloat16 or wider, within the bound.
A program may use at most 384 MiB of HBM per device.

```python
import jax
import jax.numpy as jnp
import numpy as np
from jax import lax

LEAF = 256
R = 64
NV = 32
LOCAL = 4
LISTMAX = 27
PATCH = 16
NXL = 64
NYL = 128
UPPER = 40


def near_flags(row_bits, col_bits):
    code_ids = jnp.arange(36, dtype=jnp.int32)
    code_row = code_ids // 6
    code_col = code_ids % 6
    return (code_row >= 1 + row_bits[..., None]) & (code_row <= 3 + row_bits[..., None]) & (code_col >= 1 + col_bits[..., None]) & (code_col <= 3 + col_bits[..., None])


def draw_lists(key, row_bits, col_bits):
    full_shape = row_bits.shape + (36,)
    code_ids = jnp.arange(36, dtype=jnp.int32)
    scores = jax.random.randint(key, full_shape, 0, 2 ** 20, dtype=jnp.int32) * 64 + code_ids
    scores = jnp.where(near_flags(row_bits, col_bits), 2 ** 30 + code_ids, scores)
    ordering = jnp.argsort(scores, axis=-1, stable=True)
    return ordering[..., :LISTMAX].astype(jnp.int32)


def local_bits():
    level_scale = jnp.asarray([2 ** level_index for level_index in range(LOCAL)], jnp.int32)
    leaf_row = jnp.arange(NXL, dtype=jnp.int32)[:, None, None]
    leaf_col = jnp.arange(NYL, dtype=jnp.int32)[None, :, None]
    row_bits = jnp.broadcast_to(leaf_row // level_scale % 2, (NXL, NYL, LOCAL))
    col_bits = jnp.broadcast_to(leaf_col // level_scale % 2, (NXL, NYL, LOCAL))
    return (row_bits, col_bits)


def upper_positions():
    row_list = []
    col_list = []
    grid_rows = NXL // PATCH
    grid_cols = NYL // PATCH
    while grid_rows >= 2:
        row_list.append(np.repeat(np.arange(grid_rows), grid_cols))
        col_list.append(np.tile(np.arange(grid_cols), grid_rows))
        grid_rows = grid_rows // 2
        grid_cols = grid_cols // 2
    return (np.concatenate(row_list), np.concatenate(col_list))


def draw_codes_local(key, part):
    row_bits, col_bits = local_bits()
    return draw_lists(jax.random.fold_in(key, 11), row_bits, col_bits)


def draw_counts_local(key, part):
    heat_level = jax.random.randint(jax.random.fold_in(key, 21), (NXL // PATCH, NYL // PATCH, LOCAL), 1, 5, dtype=jnp.int32)
    heat_level = jnp.repeat(jnp.repeat(heat_level, PATCH, axis=0), PATCH, axis=1)
    base_count = jax.random.randint(jax.random.fold_in(key, 22), (NXL, NYL, LOCAL), 0, LISTMAX, dtype=jnp.int32)
    return (1 + base_count * heat_level // 4).astype(jnp.int32)


def draw_codes_upper(key, part):
    row_list, col_list = upper_positions()
    row_bits = jnp.asarray(row_list % 2, jnp.int32)
    col_bits = jnp.asarray(col_list % 2, jnp.int32)
    return draw_lists(jax.random.fold_in(key, 31), row_bits, col_bits)


def draw_counts_upper(key, part):
    heat_level = jax.random.randint(jax.random.fold_in(key, 41), (UPPER,), 1, 5, dtype=jnp.int32)
    base_count = jax.random.randint(jax.random.fold_in(key, 42), (UPPER,), 0, LISTMAX, dtype=jnp.int32)
    return (1 + base_count * heat_level // 4).astype(jnp.int32)


def shard_levels(own_key, extent, shards, least, high):
    loudness, own = 1.0, jax.random.fold_in(own_key, 6)
    for position, shards_of in shards:
        steps = jnp.exp(jax.random.uniform(jax.random.fold_in(own, position), (shards_of,), jnp.float32, least / len(shards), high / len(shards)))
        loudness = loudness * jnp.repeat(steps, extent[position] // shards_of).reshape([-1 if axis == position else 1 for axis in range(len(extent))])
    return loudness


def gaussian(own_key, extent, width, most, pieces=(), kind=jnp.bfloat16):
    gain = shard_levels(own_key, extent, pieces, -0.22, 0.18) if pieces else 1.0
    values = jax.random.normal(own_key, extent, jnp.float32) * width * gain
    return jnp.minimum(jnp.maximum(values, -most), most).astype(kind)


def setup_inputs(seed: int = 0) -> dict:
    splits = jax.random.split(jax.random.key(seed), 10)
    samples = gaussian(splits[0], (NXL, NYL, NV, LEAF), 1.0, 6.0, ((0, 4), (1, 8)))
    leaf_basis = gaussian(splits[1], (R, LEAF), LEAF ** -0.5, 0.375)
    transfer = gaussian(splits[2], (LOCAL + 1, R, 4 * R), (2 * R) ** -0.5, 0.5)
    coupling = gaussian(splits[3], (LOCAL + 1, 7, R, 7 * R), (27 * R) ** -0.5, 0.15625)
    near_tiles = gaussian(splits[4], (9, LEAF, LEAF), (9 * LEAF) ** -0.5, 0.125)
    codes_local = draw_codes_local(jax.random.fold_in(splits[9], 71), 0)
    counts_local = draw_counts_local(jax.random.fold_in(splits[9], 71), 0)
    codes_upper = draw_codes_upper(jax.random.fold_in(splits[9], 71), 0)
    counts_upper = draw_counts_upper(jax.random.fold_in(splits[9], 71), 0)
    return dict(samples=samples, leaf_basis=leaf_basis, transfer=transfer, coupling=coupling, near_tiles=near_tiles, codes_local=codes_local, counts_local=counts_local, codes_upper=codes_upper, counts_upper=counts_upper)


def is_near(row_step, col_step):
    return abs(row_step) <= 1 and abs(col_step) <= 1


def lift_level(children, matrices):
    grid_rows, grid_cols, vectors, rank_size = children.shape
    grouped = children.reshape(grid_rows // 2, 2, grid_cols // 2, 2, vectors, rank_size)
    grouped = grouped.transpose(0, 2, 4, 1, 3, 5).reshape(grid_rows // 2, grid_cols // 2, vectors, 4 * rank_size)
    parent = jnp.einsum('pqvc,sc->pqvs', grouped.astype(jnp.float32), matrices.astype(jnp.float32))
    return parent.astype(jnp.bfloat16)


def spread(parent, matrices):
    grid_rows, grid_cols, vectors, rank_size = parent.shape
    carried = jnp.einsum('pqvs,sc->pqvc', parent.astype(jnp.float32), matrices.astype(jnp.float32))
    carried = carried.reshape(grid_rows, grid_cols, vectors, 2, 2, rank_size).transpose(0, 3, 1, 4, 2, 5)
    return carried.reshape(2 * grid_rows, 2 * grid_cols, vectors, rank_size)


def member_table(list_codes, counts):
    slot_index = jnp.arange(list_codes.shape[-1], dtype=jnp.int32)
    active = slot_index < counts[..., None]
    matches = (list_codes[..., None] == jnp.arange(36, dtype=jnp.int32)) & active[..., None]
    return jnp.any(matches, axis=-2).astype(jnp.float32)


def couple(padded, member, matrices):
    grid_rows = padded.shape[0] - 4
    grid_cols = padded.shape[1] - 4
    vectors = padded.shape[2]
    rank_size = padded.shape[3]
    member = member.reshape(grid_rows // 2, 2, grid_cols // 2, 2, 36)
    totals = [[jnp.zeros((grid_rows // 2, grid_cols // 2, vectors, rank_size), jnp.float32) for col_bit in range(2)] for row_bit in range(2)]
    for code_row in range(6):
        for code_col in range(6):
            parities = [(row_bit, col_bit) for row_bit in range(2) for col_bit in range(2) if not is_near(code_row - 2 - row_bit, code_col - 2 - col_bit)]
            if not parities:
                continue
            source = padded[code_row:code_row + grid_rows:2, code_col:code_col + grid_cols:2]
            blocks = jnp.concatenate([matrices[code_row + 1 - row_bit, :, (code_col + 1 - col_bit) * rank_size:(code_col + 2 - col_bit) * rank_size] for (row_bit, col_bit) in parities], axis=0)
            images = jnp.einsum('pqvr,sr->pqvs', source.astype(jnp.float32), blocks.astype(jnp.float32))
            for number, (row_bit, col_bit) in enumerate(parities):
                weight_mask = member[:, row_bit, :, col_bit, code_row * 6 + code_col]
                totals[row_bit][col_bit] = totals[row_bit][col_bit] + weight_mask[..., None, None] * images[..., number * rank_size:(number + 1) * rank_size]
    stacked = jnp.stack([jnp.stack(totals[row_bit], axis=0) for row_bit in range(2)], axis=0)
    return stacked.transpose(2, 0, 3, 1, 4, 5).reshape(grid_rows, grid_cols, vectors, rank_size)


def reference(samples, leaf_basis, transfer, coupling, near_tiles, codes_local, counts_local, codes_upper, counts_upper):
    leaf_rows = samples.shape[0]
    leaf_cols = samples.shape[1]
    row_blocks = leaf_rows // PATCH
    blocked = samples.reshape(row_blocks, PATCH, leaf_cols, NV, LEAF)

    def project(rows_block):
        return jnp.einsum('ijvs,rs->ijvr', rows_block.astype(jnp.float32), leaf_basis.astype(jnp.float32)).astype(jnp.bfloat16)

    level_coeffs = [lax.map(project, blocked).reshape(leaf_rows, leaf_cols, NV, R)]
    while level_coeffs[-1].shape[0] > 2:
        level_index = len(level_coeffs) - 1
        level_coeffs.append(lift_level(level_coeffs[-1], transfer[min(level_index, LOCAL)]))

    members = []
    offset = 0
    for level_index, coeffs in enumerate(level_coeffs):
        if level_index < LOCAL:
            stride = 2 ** level_index
            members.append(member_table(codes_local[::stride, ::stride, level_index], counts_local[::stride, ::stride, level_index]))
        else:
            grid_rows = coeffs.shape[0]
            grid_cols = coeffs.shape[1]
            count_here = grid_rows * grid_cols
            members.append(member_table(codes_upper[offset:offset + count_here].reshape(grid_rows, grid_cols, LISTMAX), counts_upper[offset:offset + count_here].reshape(grid_rows, grid_cols)))
            offset = offset + count_here

    images = []
    for level_index, coeffs in enumerate(level_coeffs):
        padded = jnp.pad(coeffs, ((2, 2), (2, 2), (0, 0), (0, 0)))
        images.append(couple(padded, members[level_index], coupling[min(level_index, LOCAL)]))
    downward = images[-1]
    for level_index in range(len(level_coeffs) - 2, -1, -1):
        downward = images[level_index] + spread(downward.astype(jnp.bfloat16), transfer[min(level_index, LOCAL)])

    padded_samples = jnp.pad(samples, ((1, 1), (1, 1), (0, 0), (0, 0)))
    far_coeffs = downward.astype(jnp.bfloat16).reshape(row_blocks, PATCH, leaf_cols, NV, R)

    def finish(inputs):
        block_index, coeffs = inputs
        window = lax.dynamic_slice_in_dim(padded_samples, block_index * PATCH, PATCH + 2, 0)
        summed = jnp.einsum('ijvr,rs->ijvs', coeffs.astype(jnp.float32), leaf_basis.astype(jnp.float32))
        for step_row in range(3):
            for step_col in range(3):
                neighbour = window[step_row:step_row + PATCH, step_col:step_col + leaf_cols]
                summed = summed + jnp.einsum('ijvs,ts->ijvt', neighbour.astype(jnp.float32), near_tiles[step_row * 3 + step_col].astype(jnp.float32))
        return summed.astype(jnp.bfloat16)

    result = lax.map(finish, (jnp.arange(row_blocks, dtype=jnp.int32), far_coeffs))
    return result.reshape(leaf_rows, leaf_cols, NV, LEAF)
```

```python
import functools

import jax
import jax.numpy as jnp
import numpy as np
from jax import lax
from jax.experimental import pallas as pl
from jax.experimental.pallas import tpu as pltpu
from jax.sharding import PartitionSpec as P

MESH = pl.DeviceIdType.MESH
F32 = jnp.float32
BF16 = jnp.bfloat16
NT = (((1,), (1,)), ((), ()))
NN = (((1,), (0,)), ((), ()))
VMEM_LIMIT = 60 * 1024 * 1024
AXES = ("gx", "gy")
SIDES = [(sx, sy) for sx in (-1, 0, 1) for sy in (-1, 0, 1) if (sx, sy) != (0, 0)]


def dot(a, b, dims):
    return lax.dot_general(a, b, dims, preferred_element_type=F32)


def twice(matrix):
    return jnp.concatenate([matrix, matrix], axis=0)


def low_half(shape, rank):
    return lax.broadcasted_iota(jnp.int32, shape, len(shape) - 1) < rank


def pair_columns(wide, vectors, rank, swap=False):
    pairs = wide.reshape(-1, 2, vectors, 2 * rank)
    even, odd = (pairs[:, 1], pairs[:, 0]) if swap else (pairs[:, 0], pairs[:, 1])
    return jnp.where(low_half(even.shape, rank), even, odd).astype(BF16)


def split_columns(paired, rank):
    count, vectors, lanes = paired.shape
    low = low_half((1, lanes), rank).astype(F32).astype(BF16)
    both = jnp.stack([paired * low, paired * (1 - low)], axis=1)
    return both.reshape(count * 2 * vectors, lanes)


def span(side, size, width):
    if side == 0:
        return pl.ds(0, size), pl.ds(width, size)
    if side > 0:
        return pl.ds(size - width, width), pl.ds(0, width)
    return pl.ds(0, width), pl.ds(width + size, width)


SHARED = 2


def far_pairs(row_bit, col_bit):
    near_rows = [1 + row_bit, 2 + row_bit, 3 + row_bit]
    far_rows = [row for row in range(6) if row not in near_rows]
    full, single = (2, 0) if col_bit == 0 else (0, 2)
    cells = [(row, pair) for row in far_rows for pair in range(3)]
    cells += [(row, full) for row in near_rows]
    entries = [("full", r, p, None, 6 * r + 2 * p, 6 * r + 2 * p + 1) for r, p in cells]
    first, last = [row for row in near_rows if row != SHARED]
    column = 0 if col_bit == 0 else 5
    codes = [6 * first + column, 6 * SHARED + column]
    low, high = codes if col_bit == 0 else codes[::-1]
    entries.append(("both", first, single, SHARED, low, high))
    code = 6 * last + column
    low, high = (code, -1) if col_bit == 0 else (-1, code)
    entries.append(("half", last, single, None, low, high))
    return entries


PARITIES = [(row_bit, col_bit) for row_bit in range(2) for col_bit in range(2)]
PAIRS = {parity: far_pairs(*parity) for parity in PARITIES}
PAIR_COUNT = len(PAIRS[0, 0])
CODE_ROWS = 48
GROUP = 128
KEPT = 96


def spread_tables(rank):
    def table(codes):
        lanes = np.repeat(np.array(codes), rank)
        return (np.arange(CODE_ROWS)[:, None] == lanes[None]).astype(np.float32)

    far = [table([c for e in PAIRS[p] for c in e[4:6]]) for p in PARITIES]
    return np.stack(far).astype(BF16), table(range(36)).astype(BF16)


def main_kernel(levels, rank, steps, counts, *refs):
    (samples_hbm, codes_hbm, counts_hbm, codes_upper_hbm, counts_upper) = refs[:5]
    (basis_hbm, transfer_hbm, coupling_hbm, table_hbm, table_upper_hbm) = refs[5:10]
    leaf_down, row_rims, col_rims = refs[10:13]
    scratch = refs[13:]
    (samples, codes, listed_counts, codes_upper) = scratch[:4]
    (basis, transfer, coupling, table, table_upper) = scratch[4:9]
    local, codes_flat, turned_counts, turned, masks, upper_masks = scratch[9:15]
    tops, zeros, send, recv, top_send, top_recv = scratch[15:21]
    scratch = scratch[21:]
    padded, swapped, images = scratch[:levels], scratch[levels : 2 * levels], scratch[2 * levels : 3 * levels]
    uppers = scratch[3 * levels : 3 * levels + steps]
    downs = (leaf_down, *scratch[3 * levels + steps :])
    patch, _, vectors, sources = samples.shape
    across, along = counts
    lanes = 2 * rank
    row_index, col_index = lax.axis_index("gx"), lax.axis_index("gy")

    chunk = 4
    fetch = [
        (codes_hbm, codes),
        (counts_hbm, listed_counts),
        (codes_upper_hbm, codes_upper),
        (coupling_hbm, coupling.at[1]),
        (basis_hbm, basis),
        (table_hbm, table),
        (table_upper_hbm, table_upper),
        (transfer_hbm, transfer),
    ]
    names = ["codes", "counts", "upper", "coupling", "basis", "table", "table_upper", "transfer"]
    fetch = {
        name: pltpu.make_async_copy(*pair, local.at[number])
        for number, (name, pair) in enumerate(zip(names, fetch))
    }

    def rows_in(number):
        spot = pl.ds(number * chunk, chunk)
        return pltpu.make_async_copy(
            samples_hbm.at[spot], samples.at[spot], local.at[len(names) + number]
        )

    for name in ("codes", "counts", "upper", "coupling", "basis"):
        fetch[name].start()
    for number in range(patch // chunk):
        rows_in(number).start()
    for name in ("table", "table_upper", "transfer"):
        fetch[name].start()

    for level in range(levels):
        target = padded[level]
        rows, cols = target.shape[:2]
        for spot in (
            (pl.ds(0, 2), pl.ds(0, cols)),
            (pl.ds(rows - 2, 2), pl.ds(0, cols)),
            (pl.ds(2, rows - 4), pl.ds(0, 1)),
            (pl.ds(2, rows - 4), pl.ds(cols - 1, 1)),
        ):
            target[spot[0], spot[1]] = jnp.zeros(
                (spot[0].size, spot[1].size, vectors, lanes), BF16
            )
    zeros[...] = jnp.zeros(zeros.shape, BF16)

    there_rows = [(row_index + step) % across for step in range(across)]
    there_cols = [(col_index + step) % along for step in range(along)]
    moves = [(dr, dc) for dr in range(across) for dc in range(along) if (dr, dc) != (0, 0)]
    barrier = pltpu.get_barrier_semaphore()
    for dr, dc in moves:
        pl.semaphore_signal(
            barrier, inc=1, device_id=(there_rows[dr], there_cols[dc]), device_id_type=MESH
        )

    def top_copy(dr, dc, from_row=None, from_col=None):
        from_row = row_index if from_row is None else from_row
        from_col = col_index if from_col is None else from_col
        return pltpu.make_async_remote_copy(
            src_ref=tops.at[row_index, col_index],
            dst_ref=tops.at[from_row, from_col],
            send_sem=top_send.at[dr * along + dc],
            recv_sem=top_recv.at[dr * along + dc],
            device_id=(there_rows[dr], there_cols[dc]),
            device_id_type=MESH,
        )

    def coeff_copy(level, number):
        sx, sy = SIDES[number]
        rows_from, rows_to = span(sx, patch >> level, 2)
        cols_from, cols_to = span(sy, patch >> (level + 1), 1)
        rows_from = pl.ds(rows_from.start + 2, rows_from.size)
        cols_from = pl.ds(cols_from.start + 1, cols_from.size)
        return pltpu.make_async_remote_copy(
            src_ref=padded[level].at[rows_from, cols_from],
            dst_ref=padded[level].at[rows_to, cols_to],
            send_sem=send.at[level, number],
            recv_sem=recv.at[level, number],
            device_id=(row_index + sx, col_index + sy),
            device_id_type=MESH,
        )

    def rim_spot(number):
        sx, sy = SIDES[number]
        _, cols_to = span(sy, patch, 1)
        if sx == 0:
            return col_rims.at[0 if sy > 0 else 1]
        return row_rims.at[pl.ds(0 if sx > 0 else 1, 1), cols_to]

    def sample_copy(number):
        sx, sy = SIDES[number]
        rows_from, _ = span(sx, patch, 1)
        cols_from, _ = span(sy, patch, 1)
        return pltpu.make_async_remote_copy(
            src_ref=samples_hbm.at[rows_from, cols_from],
            dst_ref=rim_spot(number),
            send_sem=send.at[levels, number],
            recv_sem=recv.at[levels, number],
            device_id=(row_index + sx, col_index + sy),
            device_id_type=MESH,
        )

    def zero_copy(number):
        sx, sy = SIDES[number]
        if sx == 0:
            pair = zeros.at[0], rim_spot(number).at[:, 0]
        else:
            pair = zeros.at[:, pl.ds(0, patch if sy == 0 else 1)], rim_spot(number)
        return pltpu.make_async_copy(*pair, recv.at[levels + 1, number])

    def inside(sx, sy):
        there_row, there_col = row_index + sx, col_index + sy
        return (there_row >= 0) & (there_row < across) & (there_col >= 0) & (there_col < along)

    for number, (sx, sy) in enumerate(SIDES):

        @pl.when(jnp.logical_not(inside(-sx, -sy)))
        def _():
            zero_copy(number).start()

    fetch["codes"].wait()
    fetch["counts"].wait()
    slots = codes.shape[-1]
    turned_counts[0 : listed_counts.shape[0], 0:patch] = listed_counts[...].astype(F32)
    turned_counts[...] = jnp.transpose(turned_counts[...])
    codes_flat[...] = jnp.full(codes_flat.shape, -1.0, F32)
    slot_lane = lax.broadcasted_iota(jnp.int32, (patch // 2, slots), 1).astype(F32)
    starts = [0]
    for level in range(levels):
        starts.append(starts[-1] + (patch >> (level + 1)) ** 2)
    for level in range(levels):
        size = patch >> level
        half = size // 2
        for row in range(size):
            for bit in range(2):
                begin = ((row << level) * patch + (bit << level)) * levels + level
                if half > 1:
                    listed = codes[pl.ds(begin, half, stride=levels << (level + 1)), :]
                    column = pl.ds(bit << level, half, stride=2 << level)
                else:
                    listed = codes[pl.ds(begin, 1), :]
                    column = pl.ds(bit << level, 1)
                lane = (row << level) * levels + level
                count = turned_counts[column, :][:, lane : lane + 1]
                spot = starts[level] + (row // 2) * half
                codes_flat[row % 2 * 2 + bit, spot : spot + half, 0:slots] = jnp.where(
                    slot_lane[:half] < count, listed.astype(F32), -1.0
                )
    fetch["upper"].wait()
    turns = [jnp.transpose(codes_flat[parity])[0:slots] for parity in range(4)]
    begin = 0
    upper_codes = codes_upper[...].astype(F32)
    upper_lane = lax.broadcasted_iota(jnp.int32, upper_codes.shape, 1)
    slot_row = lax.broadcasted_iota(jnp.int32, (slots, 1), 0)
    group_lane = lax.broadcasted_iota(jnp.int32, (slots, GROUP), 1)
    for step in range(steps):
        cols = along >> step
        index = begin + (row_index // 2**step) * cols + col_index // 2**step
        listed = jnp.sum(jnp.where(upper_lane == index, upper_codes, 0.0), axis=1, keepdims=True)
        listed = jnp.where(slot_row < counts_upper[index], listed, -1.0)
        turns[0] = jnp.where(group_lane == KEPT - 8 + step, listed, turns[0])
        begin += (across >> step) * cols
    for parity in range(4):
        turned[0:slots, parity * GROUP : (parity + 1) * GROUP] = turns[parity]
    code = lax.broadcasted_iota(jnp.int32, (CODE_ROWS, GROUP), 0).astype(F32)
    founds = []
    for parity in range(4):
        found = jnp.zeros((GROUP, GROUP), F32)[0:CODE_ROWS]
        for slot in range(slots):
            listed = turned[slot : slot + 1, parity * GROUP : (parity + 1) * GROUP]
            found = jnp.where(code == listed, 1.0, found)
        found = jnp.concatenate([found, jnp.zeros((GROUP - CODE_ROWS, GROUP), F32)], axis=0)
        founds.append(jnp.transpose(found)[0:KEPT, 0:CODE_ROWS].astype(BF16))
    fetch["coupling"].wait()

    def shift(level, carry):
        for part in range(coupling.shape[2]):
            coupling[0, level, part, :, 0 : 6 * rank] = coupling[1, level, part, :, rank : 7 * rank]
        return carry

    lax.fori_loop(0, coupling.shape[1], shift, 0)
    fetch["table"].wait()
    fetch["table_upper"].wait()
    for parity in range(4):
        masks[parity] = dot(founds[parity], table[parity], NN)
    upper_masks[...] = dot(founds[0][KEPT - 16 :], table_upper[...], NN)[8:]

    fetch["basis"].wait()
    own_basis = twice(basis[...])
    for number in range(patch // chunk):
        rows_in(number).wait()

    def project(number, carry):
        rows = samples[pl.ds(number * chunk, chunk)].reshape(-1, sources)
        wide = dot(rows, own_basis, NT).reshape(chunk, patch * vectors, lanes)
        for row in range(chunk):
            padded[0][number * chunk + row + 2, 1 : 1 + patch // 2] = pair_columns(
                wide[row], vectors, rank
            )
            if row % 2 == 0:
                swapped[0][number * (chunk // 2) + row // 2, 1 : 1 + patch // 2] = pair_columns(
                    wide[row], vectors, rank, True
                )
        return carry

    lax.fori_loop(0, patch // chunk, project, 0)
    pl.semaphore_wait(barrier, len(moves))

    def send_level(level):
        for number, (sx, sy) in enumerate(SIDES):

            @pl.when(inside(sx, sy))
            def _():
                coeff_copy(level, number).start()

    send_level(0)
    fetch["transfer"].wait()

    for level in range(levels):
        child = padded[level]
        matrix = twice(transfer[level])
        cols = patch >> (level + 1)
        grouped = jnp.concatenate(
            [
                jnp.concatenate(
                    [child[2 * row + 2, 1 : 1 + cols], child[2 * row + 3, 1 : 1 + cols]], axis=-1
                ).reshape(-1, 4 * rank)
                for row in range(cols)
            ],
            axis=0,
        )
        lifted = dot(grouped, matrix, NT)
        if level < levels - 1:
            lifted = lifted.reshape(cols, cols * vectors, lanes)
            for row in range(cols):
                padded[level + 1][row + 2, 1 : 1 + cols // 2] = pair_columns(
                    lifted[row], vectors, rank
                )
                if row % 2 == 0:
                    swapped[level + 1][row // 2, 1 : 1 + cols // 2] = pair_columns(
                        lifted[row], vectors, rank, True
                    )
        else:
            odd = col_index % 2
            lane = lax.broadcasted_iota(jnp.int32, lifted.shape, 1)
            own = (lane >= odd * rank) & (lane < (odd + 1) * rank)
            tops[row_index, col_index] = jnp.where(own, lifted, 0.0).astype(BF16)

    for level in range(levels - 1, 0, -1):
        send_level(level)
    for dr, dc in moves:
        top_copy(dr, dc).start()
    for number, (sx, sy) in enumerate(SIDES):

        @pl.when(inside(sx, sy))
        def _():
            sample_copy(number).start()

    low_lanes = low_half((1, lanes), rank).astype(F32).astype(BF16)
    high_lanes = 1 - low_lanes

    def weights(level, row_bit):
        sides = []
        for col_bit in range(2):
            parts = []
            for kind, row, pair, other, _, _ in PAIRS[row_bit, col_bit]:
                spot = pl.ds(pair * lanes, lanes)
                part = coupling[col_bit, level, row + 1 - row_bit, :, spot]
                if kind == "both":
                    second = coupling[1 - col_bit, level, other + 1 - row_bit, :, spot]
                    if col_bit == 0:
                        part = part * low_lanes + second * high_lanes
                    else:
                        part = part * high_lanes + second * low_lanes
                parts.append(part)
            parts = jnp.concatenate(parts, axis=-1)
            blank = jnp.zeros_like(parts)
            sides.append(jnp.concatenate([parts, blank] if col_bit == 0 else [blank, parts], axis=0))
        return jnp.concatenate(sides, axis=-1)

    def couple(level, cells):
        cols = patch >> (level + 1)
        for row_bit in range(2):
            left = []
            for row, col in cells:
                line = []
                for col_bit in range(2):
                    spot = starts[level] + row * cols + col
                    mask = masks[row_bit * 2 + col_bit, pl.ds(spot, 1), :]
                    mask = jnp.broadcast_to(mask, (16, PAIR_COUNT * lanes)).astype(BF16)
                    parts = []
                    for kind, part_row, pair, _, _, _ in PAIRS[row_bit, col_bit]:
                        part = padded[level][2 * row + part_row, col + pair]
                        if kind == "both":
                            second = swapped[level][row, col + pair]
                            if col_bit == 0:
                                part = part * low_lanes + second * high_lanes
                            else:
                                part = part * high_lanes + second * low_lanes
                        parts.append(part)
                    parts = jnp.concatenate(parts, axis=-1)
                    parts = parts.reshape(-1, 16, PAIR_COUNT * lanes) * mask[None]
                    line.append(parts.reshape(vectors, PAIR_COUNT * lanes))
                left.append(jnp.concatenate(line, axis=-1))
            image = dot(jnp.concatenate(left, axis=0), weights(level, row_bit), NT)
            image = image.reshape(len(cells), vectors, lanes)
            for number, (row, col) in enumerate(cells):
                images[level][2 * row + row_bit, col] = image[number]

    inner = range(1, patch // 2 - 1)

    def inner_rows(pair, carry):
        couple(0, [(1 + 2 * pair + step, col) for step in range(2) for col in inner])
        return carry

    lax.fori_loop(0, len(inner) // 2, inner_rows, 0)

    for level in range(levels):
        for number, (sx, sy) in enumerate(SIDES):

            @pl.when(inside(-sx, -sy))
            def _():
                coeff_copy(level, number).wait_recv()

    for level in range(levels):
        rows, cols = patch >> (level + 1), (patch >> (level + 1)) + 2
        for edge in (0, cols - 1):
            for row in range(rows):
                piece = padded[level][2 * row + 2, edge].astype(F32)
                swapped[level][row, edge] = pltpu.roll(piece, rank, 1).astype(BF16)

    last = patch // 2 - 1
    couple(0, [(row, col) for row in (0, last) for col in range(patch // 2)])
    couple(0, [(row, col) for row in inner for col in (0, last)])
    for level in range(1, levels):
        size = patch >> (level + 1)
        couple(level, [(row, col) for row in range(size) for col in range(size)])

    for dr, dc in moves:
        top_copy(dr, dc, (row_index - dr) % across, (col_index - dc) % along).wait_recv()

    def window(ref, row, col):
        return jnp.concatenate(
            [ref[row + code, col + step] for code in range(6) for step in range(3)], axis=-1
        )

    uppers[0][...] = jnp.zeros(uppers[0].shape, BF16)
    for row in range(across):
        for col in range(along // 2):
            uppers[0][row + 2, col + 1] = tops[row, 2 * col] + tops[row, 2 * col + 1]
    top_matrix = twice(transfer[levels])
    for step in range(steps - 1):
        child, parent = uppers[step], uppers[step + 1]
        parent[...] = jnp.zeros(parent.shape, BF16)
        rows, cols = across >> step, along >> (step + 1)
        grouped = jnp.concatenate(
            [
                jnp.concatenate(
                    [child[2 * row + 2, 1 : 1 + cols], child[2 * row + 3, 1 : 1 + cols]], axis=-1
                ).reshape(-1, 4 * rank)
                for row in range(rows // 2)
            ],
            axis=0,
        )
        lifted = dot(grouped, top_matrix, NT).reshape(rows // 2, cols * vectors, lanes)
        for row in range(rows // 2):
            parent[row + 2, 1 : 1 + cols // 2] = pair_columns(lifted[row], vectors, rank)
    low = low_half((vectors, lanes), rank)
    upper_images = []
    for step in range(steps):
        row, col = row_index // 2**step, col_index // 2**step
        slab = window(uppers[step], 2 * (row // 2), col // 2)
        mask = jnp.broadcast_to(upper_masks[step : step + 1, :], (16, 36 * rank)).astype(BF16)
        slab = (slab.reshape(-1, 16, 36 * rank) * mask[None]).reshape(slab.shape)
        flat = jnp.concatenate(
            [coupling[col % 2, levels, code + 1 - row % 2, :, 0 : 6 * rank] for code in range(6)],
            axis=-1,
        )
        upper_images.append(dot(slab, twice(flat), NT))
    down = upper_images[-1]
    for step in range(steps - 2, -1, -1):
        row, col = row_index // 2**step, col_index // 2**step
        carried = dot(down.astype(BF16) * low_lanes, top_matrix, NN)
        part = jnp.where(row % 2 == 0, carried[:, :lanes], carried[:, lanes:])
        part = jnp.where(low == (col % 2 == 0), part, pltpu.roll(part, rank, 1))
        down = upper_images[step] + part

    for level in range(levels - 1, -1, -1):
        size = patch >> (level + 1)
        if level == levels - 1:
            parent = down.astype(BF16) * low_lanes
        else:
            parent = jnp.concatenate(
                [split_columns(downs[level + 1][row], rank) for row in range(size)], axis=0
            )
        carried = dot(parent, twice(transfer[level]), NN)
        carried = carried.reshape(size, size, vectors, 2 * lanes)
        for row in range(size):
            for row_bit in range(2):
                spot = 2 * row + row_bit
                part = carried[row, :, :, row_bit * lanes : (row_bit + 1) * lanes]
                downs[level][spot] = (images[level][spot] + part).astype(BF16)

    for number, (sx, sy) in enumerate(SIDES):

        @pl.when(inside(-sx, -sy))
        def _():
            sample_copy(number).wait_recv()

        @pl.when(jnp.logical_not(inside(-sx, -sy)))
        def _():
            zero_copy(number).wait()

        @pl.when(inside(sx, sy))
        def _():
            for level in range(levels):
                coeff_copy(level, number).wait_send()
            sample_copy(number).wait_send()

    for dr, dc in moves:
        top_copy(dr, dc).wait_send()


def finish_kernel(strip, rank, *refs):
    samples_hbm, row_rims, col_rims, near_hbm, down_hbm, basis_hbm, out_hbm = refs[:7]
    samples, near, down, basis, out, rows_sem, out_sem, sems = refs[7:]
    patch, _, vectors, sources = out.shape

    def rows_in(row):
        return pltpu.make_async_copy(
            samples_hbm.at[row], samples.at[row + 1, pl.ds(1, patch)], rows_sem.at[row]
        )

    inner = pl.ds(1, patch)
    fetch = [
        (near_hbm, near),
        (basis_hbm, basis),
        (row_rims.at[0], samples.at[0]),
        (col_rims.at[0], samples.at[inner, pl.ds(0, 1)]),
        (col_rims.at[1], samples.at[inner, pl.ds(patch + 1, 1)]),
        (down_hbm, down),
        (row_rims.at[1], samples.at[patch + 1]),
    ]
    fetch = [pltpu.make_async_copy(*pair, sems.at[n]) for n, pair in enumerate(fetch)]
    for copy in fetch[:5]:
        copy.start()
    for row in range(patch):
        rows_in(row).start()
        if row == strip:
            fetch[5].start()
    fetch[6].start()
    for copy in fetch[:6]:
        copy.wait()
    for row in range(strip):
        rows_in(row).wait()
    basis2 = twice(basis[...])

    def rows_out(number):
        spot = pl.ds(number * strip, strip)
        return pltpu.make_async_copy(out.at[spot], out_hbm.at[spot], out_sem.at[number])

    def body(number, carry):
        begin = number * strip

        @pl.when(begin + strip < patch)
        def _():
            for row in range(strip):
                rows_in(begin + strip + row).wait()

        @pl.when(begin + strip >= patch)
        def _():
            fetch[6].wait()

        left = jnp.concatenate(
            [
                samples[pl.ds(begin + row, strip), col : col + patch].reshape(-1, sources)
                for row in range(3)
                for col in range(3)
            ],
            axis=-1,
        )
        flat = jnp.concatenate([near[tile] for tile in range(9)], axis=-1)
        far = split_columns(down[pl.ds(begin, strip)].reshape(-1, vectors, 2 * rank), rank)
        summed = dot(left, flat, NT) + dot(far, basis2, NN)
        out[pl.ds(begin, strip)] = summed.astype(BF16).reshape(strip, patch, vectors, sources)
        rows_out(number).start()
        return carry

    lax.fori_loop(0, patch // strip, body, 0)

    def end(number, carry):
        rows_out(number).wait()
        return carry

    lax.fori_loop(0, patch // strip, end, 0)


def shards(
    samples,
    leaf_basis,
    transfer,
    coupling,
    near_tiles,
    codes_local,
    counts_local,
    codes_upper,
    counts_upper,
):
    patch, _, vectors, sources = samples.shape
    rank = leaf_basis.shape[0]
    levels = transfer.shape[0] - 1
    lanes = 2 * rank
    across, along = lax.axis_size("gx"), lax.axis_size("gy")
    steps = 1
    while across >> steps >= 2:
        steps += 1
    hbm = pl.BlockSpec(memory_space=pltpu.MemorySpace.HBM)
    vmem = pl.BlockSpec(memory_space=pltpu.VMEM)
    slots = codes_local.shape[-1]
    codes = codes_local.reshape(-1, slots)
    listed_counts = counts_local.transpose(0, 2, 1).reshape(-1, patch)
    far_table, upper_table = spread_tables(rank)

    shapes = [(patch >> level, patch >> (level + 1), vectors, lanes) for level in range(levels)]
    leaf_down, row_rims, col_rims = pl.pallas_call(
        functools.partial(main_kernel, levels, rank, steps, (across, along)),
        out_shape=[
            jax.ShapeDtypeStruct(shapes[0], BF16),
            jax.ShapeDtypeStruct((2, patch + 2, vectors, sources), BF16),
            jax.ShapeDtypeStruct((2, patch, 1, vectors, sources), BF16),
        ],
        in_specs=[hbm] * 4 + [pl.BlockSpec(memory_space=pltpu.SMEM)] + [hbm] * 5,
        out_specs=[vmem, hbm, hbm],
        scratch_shapes=[
            pltpu.VMEM(samples.shape, BF16),
            pltpu.VMEM(codes.shape, jnp.int32),
            pltpu.VMEM(listed_counts.shape, jnp.int32),
            pltpu.VMEM(codes_upper.shape[::-1], jnp.int32),
            pltpu.VMEM(leaf_basis.shape, BF16),
            pltpu.VMEM(transfer.shape, BF16),
            pltpu.VMEM((2, *coupling.shape), BF16),
            pltpu.VMEM(far_table.shape, BF16),
            pltpu.VMEM(upper_table.shape, BF16),
            pltpu.SemaphoreType.DMA((8 + patch // 4,)),
            pltpu.VMEM((4, GROUP, GROUP), F32),
            pltpu.VMEM((GROUP, GROUP), F32),
            pltpu.VMEM((32, 4 * GROUP), F32),
            pltpu.VMEM((4, KEPT, PAIR_COUNT * lanes), F32),
            pltpu.VMEM((8, 36 * rank), F32),
            pltpu.VMEM((across, along, vectors, lanes), BF16),
            pltpu.VMEM((1, patch, vectors, sources), BF16),
            pltpu.SemaphoreType.DMA((levels + 1, len(SIDES))),
            pltpu.SemaphoreType.DMA((levels + 2, len(SIDES))),
            pltpu.SemaphoreType.DMA((across * along,)),
            pltpu.SemaphoreType.DMA((across * along,)),
        ]
        + [pltpu.VMEM((rows + 4, cols + 2, vectors, lanes), BF16) for rows, cols, _, _ in shapes]
        + [pltpu.VMEM((rows // 2, cols + 2, vectors, lanes), BF16) for rows, cols, _, _ in shapes]
        + [pltpu.VMEM(shape, F32) for shape in shapes]
        + [
            pltpu.VMEM(((across >> step) + 4, (along >> (step + 1)) + 2, vectors, lanes), BF16)
            for step in range(steps)
        ]
        + [pltpu.VMEM(shape, BF16) for shape in shapes[1:]],
        compiler_params=pltpu.CompilerParams(
            collective_id=0, has_side_effects=True, vmem_limit_bytes=VMEM_LIMIT
        ),
        name="main",
    )(
        samples,
        codes,
        listed_counts,
        codes_upper.T,
        counts_upper,
        leaf_basis,
        transfer,
        coupling,
        jnp.asarray(far_table),
        jnp.asarray(upper_table),
    )
    strip = 2
    return pl.pallas_call(
        functools.partial(finish_kernel, strip, rank),
        out_shape=jax.ShapeDtypeStruct(samples.shape, BF16),
        in_specs=[hbm] * 6,
        out_specs=hbm,
        scratch_shapes=[
            pltpu.VMEM((patch + 2, patch + 2, vectors, sources), BF16),
            pltpu.VMEM(near_tiles.shape, BF16),
            pltpu.VMEM(shapes[0], BF16),
            pltpu.VMEM(leaf_basis.shape, BF16),
            pltpu.VMEM(samples.shape, BF16),
            pltpu.SemaphoreType.DMA((patch,)),
            pltpu.SemaphoreType.DMA((patch // strip,)),
            pltpu.SemaphoreType.DMA((7,)),
        ],
        compiler_params=pltpu.CompilerParams(vmem_limit_bytes=VMEM_LIMIT),
        name="finish",
    )(samples, row_rims, col_rims, near_tiles, leaf_down, leaf_basis)


def solution(mesh):
    placed = (
        P("gx", "gy", None, None),
        P(),
        P(),
        P(),
        P(),
        P("gx", "gy", None, None),
        P("gx", "gy", None),
        P(),
        P(),
    )
    return jax.shard_map(
        shards, mesh=mesh, in_specs=placed, out_specs=P("gx", "gy", None, None), check_vma=False
    )
```

```python
import functools

import jax
import jax.numpy as jnp
import numpy as np
from jax import lax
from jax.experimental import pallas as pl
from jax.experimental.pallas import tpu as pltpu
from jax.sharding import PartitionSpec as P

MESH = pl.DeviceIdType.MESH
F32 = jnp.float32
BF16 = jnp.bfloat16
NT = (((1,), (1,)), ((), ()))
NN = (((1,), (0,)), ((), ()))
VMEM_LIMIT = 60 * 1024 * 1024
AXES = ("gx", "gy")
SIDES = [(sx, sy) for sx in (-1, 0, 1) for sy in (-1, 0, 1) if (sx, sy) != (0, 0)]


def dot(a, b, dims):
    return lax.dot_general(a, b, dims, preferred_element_type=F32)


def twice(matrix):
    return jnp.concatenate([matrix, matrix], axis=0)


def low_half(shape, rank):
    return lax.broadcasted_iota(jnp.int32, shape, len(shape) - 1) < rank


def pair_columns(wide, vectors, rank, swap=False):
    pairs = wide.reshape(-1, 2, vectors, 2 * rank)
    even, odd = (pairs[:, 1], pairs[:, 0]) if swap else (pairs[:, 0], pairs[:, 1])
    return jnp.where(low_half(even.shape, rank), even, odd).astype(BF16)


def split_columns(paired, rank):
    count, vectors, lanes = paired.shape
    low = low_half((1, lanes), rank).astype(F32).astype(BF16)
    both = jnp.stack([paired * low, paired * (1 - low)], axis=1)
    return both.reshape(count * 2 * vectors, lanes)


def span(side, size, width):
    if side == 0:
        return pl.ds(0, size), pl.ds(width, size)
    if side > 0:
        return pl.ds(size - width, width), pl.ds(0, width)
    return pl.ds(0, width), pl.ds(width + size, width)


SHARED = 2


def far_pairs(row_bit, col_bit):
    near_rows = [1 + row_bit, 2 + row_bit, 3 + row_bit]
    far_rows = [row for row in range(6) if row not in near_rows]
    full, single = (2, 0) if col_bit == 0 else (0, 2)
    cells = [(row, pair) for row in far_rows for pair in range(3)]
    cells += [(row, full) for row in near_rows]
    entries = [("full", r, p, None, 6 * r + 2 * p, 6 * r + 2 * p + 1) for r, p in cells]
    first, last = [row for row in near_rows if row != SHARED]
    column = 0 if col_bit == 0 else 5
    codes = [6 * first + column, 6 * SHARED + column]
    low, high = codes if col_bit == 0 else codes[::-1]
    entries.append(("both", first, single, SHARED, low, high))
    code = 6 * last + column
    low, high = (code, -1) if col_bit == 0 else (-1, code)
    entries.append(("half", last, single, None, low, high))
    return entries


PARITIES = [(row_bit, col_bit) for row_bit in range(2) for col_bit in range(2)]
PAIRS = {parity: far_pairs(*parity) for parity in PARITIES}
PAIR_COUNT = len(PAIRS[0, 0])
CODE_ROWS = 48
GROUP = 128
KEPT = 96


def spread_tables(rank):
    def table(codes):
        lanes = np.repeat(np.array(codes), rank)
        return (np.arange(CODE_ROWS)[:, None] == lanes[None]).astype(np.float32)

    far = [table([c for e in PAIRS[p] for c in e[4:6]]) for p in PARITIES]
    return np.stack(far).astype(BF16), table(range(36)).astype(BF16)


def main_kernel(levels, rank, steps, counts, *refs):
    (samples_hbm, codes_hbm, counts_hbm, codes_upper_hbm, counts_upper) = refs[:5]
    (basis_hbm, transfer_hbm, coupling_hbm, table_hbm, table_upper_hbm) = refs[5:10]
    down_hbm, row_rims, col_rims = refs[10:13]
    scratch = refs[13:]
    (samples, codes, listed_counts, codes_upper) = scratch[:4]
    (basis, transfer, coupling, table, table_upper) = scratch[4:9]
    local, codes_flat, turned_counts, turned, masks, upper_masks = scratch[9:15]
    tops, zeros, send, recv, top_send, top_recv = scratch[15:21]
    scratch = scratch[21:]
    padded, swapped, images = scratch[:levels], scratch[levels : 2 * levels], scratch[2 * levels : 3 * levels]
    uppers = scratch[3 * levels : 3 * levels + steps]
    downs = scratch[3 * levels + steps :]
    patch, _, vectors, sources = samples.shape
    across, along = counts
    lanes = 2 * rank
    row_index, col_index = lax.axis_index("gx"), lax.axis_index("gy")

    chunk = 4
    fetch = [
        (codes_hbm, codes),
        (counts_hbm, listed_counts),
        (codes_upper_hbm, codes_upper),
        (coupling_hbm, coupling.at[1]),
        (basis_hbm, basis),
        (table_hbm, table),
        (table_upper_hbm, table_upper),
        (transfer_hbm, transfer),
    ]
    names = ["codes", "counts", "upper", "coupling", "basis"]
    names += ["table", "table_upper", "transfer"]
    fetch = {
        name: pltpu.make_async_copy(*pair, local.at[number])
        for number, (name, pair) in enumerate(zip(names, fetch))
    }

    def rows_in(number):
        spot = pl.ds(number * chunk, chunk)
        return pltpu.make_async_copy(
            samples_hbm.at[spot], samples.at[spot], local.at[len(names) + number]
        )

    for name in ("codes", "counts", "upper", "basis"):
        fetch[name].start()
    for number in range(patch // chunk):
        rows_in(number).start()
    for name in ("transfer", "coupling", "table", "table_upper"):
        fetch[name].start()

    def clear_border(target, height, width):
        rows, cols, *tail = target.shape
        for top, tall, left, wide in (
            (0, height, 0, cols),
            (rows - height, height, 0, cols),
            (height, rows - 2 * height, 0, width),
            (height, rows - 2 * height, cols - width, width),
        ):
            target[top : top + tall, left : left + wide] = jnp.zeros((tall, wide, *tail), BF16)

    zeros[...] = jnp.zeros(zeros.shape, BF16)
    for level in range(levels):
        clear_border(padded[level], 2, 1)

    there_rows = [(row_index + step) % across for step in range(across)]
    there_cols = [(col_index + step) % along for step in range(along)]
    moves = [(dr, dc) for dr in range(across) for dc in range(along) if (dr, dc) != (0, 0)]
    barrier = pltpu.get_barrier_semaphore()
    for dr, dc in moves:
        pl.semaphore_signal(
            barrier, inc=1, device_id=(there_rows[dr], there_cols[dc]), device_id_type=MESH
        )

    def top_copy(dr, dc, from_row=None, from_col=None):
        from_row = row_index if from_row is None else from_row
        from_col = col_index if from_col is None else from_col
        return pltpu.make_async_remote_copy(
            src_ref=tops.at[row_index, col_index],
            dst_ref=tops.at[from_row, from_col],
            send_sem=top_send.at[dr * along + dc],
            recv_sem=top_recv.at[dr * along + dc],
            device_id=(there_rows[dr], there_cols[dc]),
            device_id_type=MESH,
        )

    def halo_copy(level, number):
        sx, sy = SIDES[number]
        ref = padded[level]
        rows_from, rows_to = span(sx, patch >> level, 2)
        cols_from, cols_to = span(sy, patch >> (level + 1), 1)
        rows_from = pl.ds(rows_from.start + 2, rows_from.size)
        corner = sx != 0 and sy != 0
        cols_from = cols_to if corner else pl.ds(cols_from.start + 1, cols_from.size)
        return pltpu.make_async_remote_copy(
            src_ref=ref.at[rows_from, cols_from],
            dst_ref=ref.at[rows_to, cols_to],
            send_sem=send.at[level, number],
            recv_sem=recv.at[level, number],
            device_id=(row_index + sx, col_index if corner else col_index + sy),
            device_id_type=MESH,
        )

    def rim_spot(number, late):
        sx, sy = SIDES[number]
        _, cols_to = span(sy, patch, 1)
        if sx == 0:
            return col_rims.at[0 if sy > 0 else 1, pl.ds(late * (patch // 2), patch // 2)]
        return row_rims.at[pl.ds(0 if sx > 0 else 1, 1), cols_to]

    def sample_copy(number, late):
        sx, sy = SIDES[number]
        rows_from, _ = span(sx, patch, 1)
        cols_from, _ = span(sy, patch, 1)
        if sx == 0:
            rows_from = pl.ds(late * (patch // 2), patch // 2)
        return pltpu.make_async_remote_copy(
            src_ref=samples_hbm.at[rows_from, cols_from],
            dst_ref=rim_spot(number, late),
            send_sem=send.at[levels + late, number],
            recv_sem=recv.at[levels + late, number],
            device_id=(row_index + sx, col_index + sy),
            device_id_type=MESH,
        )

    def zero_copy(number, late):
        sx, sy = SIDES[number]
        if sx == 0:
            pair = zeros.at[0, pl.ds(0, patch // 2)], rim_spot(number, late).at[:, 0]
        else:
            pair = zeros.at[:, pl.ds(0, patch if sy == 0 else 1)], rim_spot(number, late)
        return pltpu.make_async_copy(*pair, recv.at[levels + 2 + late, number])

    def inside(sx, sy):
        there_row, there_col = row_index + sx, col_index + sy
        return (there_row >= 0) & (there_row < across) & (there_col >= 0) & (there_col < along)

    numbered = list(enumerate(SIDES))
    column_sides = [n for n, (sx, sy) in numbered if sx == 0]
    row_sides = [n for n, (sx, sy) in numbered if sy == 0]
    corners = [n for n, (sx, sy) in numbered if sx != 0 and sy != 0]

    def sends(number):
        sx, sy = SIDES[number]
        return inside(sx, 0) & inside(0, -sy) if number in corners else inside(sx, sy)

    early = column_sides + row_sides
    late = column_sides + corners

    def start_samples(numbers, is_late):
        for number in numbers:

            @pl.when(inside(*SIDES[number]))
            def _():
                sample_copy(number, is_late).start()

    for is_late, numbers in enumerate((early, late)):
        for number in numbers:
            sx, sy = SIDES[number]

            @pl.when(jnp.logical_not(inside(-sx, -sy)))
            def _():
                zero_copy(number, is_late).start()

    def start_halo(which, numbers):
        for number in numbers:

            @pl.when(sends(number))
            def _():
                for level in which:
                    halo_copy(level, number).start()

    def wait_halo(which, numbers):
        for number in numbers:
            sx, sy = SIDES[number]

            @pl.when(inside(-sx, -sy))
            def _():
                for level in which:
                    halo_copy(level, number).wait_recv()

    fetch["codes"].wait()
    fetch["counts"].wait()
    slots = codes.shape[-1]
    turned_counts[0 : listed_counts.shape[0], 0:patch] = listed_counts[...].astype(F32)
    turned_counts[...] = jnp.transpose(turned_counts[...])
    codes_flat[...] = jnp.full(codes_flat.shape, -1.0, F32)
    slot_lane = lax.broadcasted_iota(jnp.int32, (patch // 2, slots), 1).astype(F32)
    starts = [0]
    for level in range(levels):
        starts.append(starts[-1] + (patch >> (level + 1)) ** 2)
    for level in range(levels):
        size = patch >> level
        half = size // 2
        for row in range(size):
            for bit in range(2):
                begin = ((row << level) * patch + (bit << level)) * levels + level
                if half > 1:
                    listed = codes[pl.ds(begin, half, stride=levels << (level + 1)), :]
                    column = pl.ds(bit << level, half, stride=2 << level)
                else:
                    listed = codes[pl.ds(begin, 1), :]
                    column = pl.ds(bit << level, 1)
                lane = (row << level) * levels + level
                count = turned_counts[column, :][:, lane : lane + 1]
                spot = starts[level] + (row // 2) * half
                codes_flat[row % 2 * 2 + bit, spot : spot + half, 0:slots] = jnp.where(
                    slot_lane[:half] < count, listed.astype(F32), -1.0
                )
    pl.semaphore_wait(barrier, len(moves))
    start_samples(early, 0)

    fetch["basis"].wait()
    own_basis = twice(basis[...])

    def project(number, carry):
        rows_in(number).wait()
        rows = samples[pl.ds(number * chunk, chunk)].reshape(-1, sources)
        wide = dot(rows, own_basis, NT).reshape(chunk, patch * vectors, lanes)
        for row in range(chunk):
            padded[0][number * chunk + row + 2, 1 : 1 + patch // 2] = pair_columns(
                wide[row], vectors, rank
            )
            if row % 2 == 0:
                swapped[0][number * (chunk // 2) + row // 2, 1 : 1 + patch // 2] = pair_columns(
                    wide[row], vectors, rank, True
                )
        return carry

    lax.fori_loop(0, patch // chunk, project, 0)
    start_halo([0], column_sides + row_sides)
    fetch["transfer"].wait()

    for level in range(levels):
        child = padded[level]
        matrix = twice(transfer[level])
        cols = patch >> (level + 1)
        grouped = jnp.concatenate(
            [
                jnp.concatenate(
                    [child[2 * row + 2, 1 : 1 + cols], child[2 * row + 3, 1 : 1 + cols]], axis=-1
                ).reshape(-1, 4 * rank)
                for row in range(cols)
            ],
            axis=0,
        )
        lifted = dot(grouped, matrix, NT)
        if level < levels - 1:
            lifted = lifted.reshape(cols, cols * vectors, lanes)
            for row in range(cols):
                padded[level + 1][row + 2, 1 : 1 + cols // 2] = pair_columns(
                    lifted[row], vectors, rank
                )
                if row % 2 == 0:
                    swapped[level + 1][row // 2, 1 : 1 + cols // 2] = pair_columns(
                        lifted[row], vectors, rank, True
                    )
        else:
            half = vectors // 2
            tops[row_index, col_index] = jnp.where(
                low_half((half, lanes), rank), lifted[:half], lifted[half:]
            ).astype(BF16)

    start_halo(range(levels - 1, 0, -1), column_sides + row_sides)
    for dr, dc in moves:
        top_copy(dr, dc).start()
    start_samples(late, 1)

    fetch["upper"].wait()
    turns = [jnp.transpose(codes_flat[parity])[0:slots] for parity in range(4)]
    begin = 0
    upper_codes = codes_upper[...].astype(F32)
    upper_lane = lax.broadcasted_iota(jnp.int32, upper_codes.shape, 1)
    slot_row = lax.broadcasted_iota(jnp.int32, (slots, 1), 0)
    group_lane = lax.broadcasted_iota(jnp.int32, (slots, GROUP), 1)
    for step in range(steps):
        cols = along >> step
        index = begin + (row_index // 2**step) * cols + col_index // 2**step
        listed = jnp.sum(jnp.where(upper_lane == index, upper_codes, 0.0), axis=1, keepdims=True)
        listed = jnp.where(slot_row < counts_upper[index], listed, -1.0)
        turns[0] = jnp.where(group_lane == KEPT - 8 + step, listed, turns[0])
        begin += (across >> step) * cols
    for parity in range(4):
        turned[0:slots, parity * GROUP : (parity + 1) * GROUP] = turns[parity]
    code = lax.broadcasted_iota(jnp.int32, (CODE_ROWS, GROUP), 0).astype(F32)
    founds = []
    for parity in range(4):
        found = jnp.zeros((GROUP, GROUP), F32)[0:CODE_ROWS]
        for slot in range(slots):
            listed = turned[slot : slot + 1, parity * GROUP : (parity + 1) * GROUP]
            found = jnp.where(code == listed, 1.0, found)
        found = jnp.concatenate([found, jnp.zeros((GROUP - CODE_ROWS, GROUP), F32)], axis=0)
        founds.append(jnp.transpose(found)[0:KEPT, 0:CODE_ROWS].astype(BF16))
    fetch["coupling"].wait()

    def shift(level, carry):
        for part in range(coupling.shape[2]):
            coupling[0, level, part, :, 0 : 6 * rank] = coupling[1, level, part, :, rank : 7 * rank]
        return carry

    lax.fori_loop(0, coupling.shape[1], shift, 0)
    fetch["table"].wait()
    fetch["table_upper"].wait()
    for parity in range(4):
        masks[parity] = dot(founds[parity], table[parity], NN)
    upper_masks[...] = dot(founds[0][KEPT - 16 :], table_upper[...], NN)[8:]

    low_lanes = low_half((1, lanes), rank).astype(F32).astype(BF16)
    high_lanes = 1 - low_lanes

    def weights(level, row_bit):
        sides = []
        for col_bit in range(2):
            parts = []
            for kind, row, pair, other, _, _ in PAIRS[row_bit, col_bit]:
                spot = pl.ds(pair * lanes, lanes)
                part = coupling[col_bit, level, row + 1 - row_bit, :, spot]
                if kind == "both":
                    second = coupling[1 - col_bit, level, other + 1 - row_bit, :, spot]
                    if col_bit == 0:
                        part = part * low_lanes + second * high_lanes
                    else:
                        part = part * high_lanes + second * low_lanes
                parts.append(part)
            parts = jnp.concatenate(parts, axis=-1)
            blank = jnp.zeros_like(parts)
            sides.append(jnp.concatenate([parts, blank] if col_bit == 0 else [blank, parts], axis=0))
        return jnp.concatenate(sides, axis=-1)

    def couple(level, cells):
        cols = patch >> (level + 1)
        for row_bit in range(2):
            left = []
            for row, col in cells:
                line = []
                for col_bit in range(2):
                    spot = starts[level] + row * cols + col
                    mask = masks[row_bit * 2 + col_bit, pl.ds(spot, 1), :]
                    mask = jnp.broadcast_to(mask, (16, PAIR_COUNT * lanes)).astype(BF16)
                    parts = []
                    for kind, part_row, pair, _, _, _ in PAIRS[row_bit, col_bit]:
                        part = padded[level][2 * row + part_row, col + pair]
                        if kind == "both":
                            second = swapped[level][row, col + pair]
                            if col_bit == 0:
                                part = part * low_lanes + second * high_lanes
                            else:
                                part = part * high_lanes + second * low_lanes
                        parts.append(part)
                    parts = jnp.concatenate(parts, axis=-1)
                    parts = parts.reshape(-1, 16, PAIR_COUNT * lanes) * mask[None]
                    line.append(parts.reshape(vectors, PAIR_COUNT * lanes))
                left.append(jnp.concatenate(line, axis=-1))
            image = dot(jnp.concatenate(left, axis=0), weights(level, row_bit), NT)
            image = image.reshape(len(cells), vectors, lanes)
            for number, (row, col) in enumerate(cells):
                images[level][2 * row + row_bit, col] = image[number]

    inner = range(1, patch // 2 - 1)

    def inner_rows(pair, carry):
        couple(0, [(1 + 2 * pair + step, col) for step in range(2) for col in inner])
        return carry

    lax.fori_loop(0, len(inner) // 2, inner_rows, 0)

    last = patch // 2 - 1
    own = range(levels)
    wait_halo([0], row_sides)
    couple(0, [(row, col) for row in (0, last) for col in inner])
    wait_halo(own, column_sides)
    start_halo(own, corners)
    for level in range(levels):
        rows, cols = patch >> (level + 1), (patch >> (level + 1)) + 2
        for edge in (0, cols - 1):
            for row in range(rows):
                piece = padded[level][2 * row + 2, edge].astype(F32)
                swapped[level][row, edge] = pltpu.roll(piece, rank, 1).astype(BF16)

    wait_halo(range(1, levels), row_sides)
    wait_halo(own, corners)
    couple(0, [(row, col) for row in range(patch // 2) for col in (0, last)])
    for level in range(1, levels):
        size = patch >> (level + 1)
        couple(level, [(row, col) for row in range(size) for col in range(size)])

    for dr, dc in moves:
        top_copy(dr, dc, (row_index - dr) % across, (col_index - dc) % along).wait_recv()

    def window(ref, row, col):
        return jnp.concatenate(
            [ref[row + code, col + step] for code in range(6) for step in range(3)], axis=-1
        )

    uppers[0][...] = jnp.zeros(uppers[0].shape, BF16)
    for row in range(across):
        for col in range(along // 2):
            even, odd = (tops[row, 2 * col + bit].astype(F32) for bit in range(2))
            low = low_half(even.shape, rank)
            first = jnp.where(low, even, pltpu.roll(odd, rank, 1))
            second = jnp.where(low, pltpu.roll(even, rank, 1), odd)
            both = jnp.concatenate([first, second], axis=0)
            uppers[0][row + 2, col + 1] = both.astype(BF16)
    top_matrix = twice(transfer[levels])
    for step in range(steps - 1):
        child, parent = uppers[step], uppers[step + 1]
        parent[...] = jnp.zeros(parent.shape, BF16)
        rows, cols = across >> step, along >> (step + 1)
        grouped = jnp.concatenate(
            [
                jnp.concatenate(
                    [child[2 * row + 2, 1 : 1 + cols], child[2 * row + 3, 1 : 1 + cols]], axis=-1
                ).reshape(-1, 4 * rank)
                for row in range(rows // 2)
            ],
            axis=0,
        )
        lifted = dot(grouped, top_matrix, NT).reshape(rows // 2, cols * vectors, lanes)
        for row in range(rows // 2):
            parent[row + 2, 1 : 1 + cols // 2] = pair_columns(lifted[row], vectors, rank)
    low = low_half((vectors, lanes), rank)
    upper_images = []
    for step in range(steps):
        row, col = row_index // 2**step, col_index // 2**step
        slab = window(uppers[step], 2 * (row // 2), col // 2)
        mask = jnp.broadcast_to(upper_masks[step : step + 1, :], (16, 36 * rank)).astype(BF16)
        slab = (slab.reshape(-1, 16, 36 * rank) * mask[None]).reshape(slab.shape)
        flat = jnp.concatenate(
            [coupling[col % 2, levels, code + 1 - row % 2, :, 0 : 6 * rank] for code in range(6)],
            axis=-1,
        )
        upper_images.append(dot(slab, twice(flat), NT))
    down = upper_images[-1]
    for step in range(steps - 2, -1, -1):
        row, col = row_index // 2**step, col_index // 2**step
        carried = dot(down.astype(BF16) * low_lanes, top_matrix, NN)
        part = jnp.where(row % 2 == 0, carried[:, :lanes], carried[:, lanes:])
        part = jnp.where(low == (col % 2 == 0), part, pltpu.roll(part, rank, 1))
        down = upper_images[step] + part

    for level in range(levels - 1, -1, -1):
        size = patch >> (level + 1)
        if level == levels - 1:
            parent = down.astype(BF16) * low_lanes
        else:
            parent = jnp.concatenate(
                [split_columns(downs[level + 1][row], rank) for row in range(size)], axis=0
            )
        carried = dot(parent, twice(transfer[level]), NN)
        carried = carried.reshape(size, size, vectors, 2 * lanes)
        for row in range(size):
            for row_bit in range(2):
                spot = 2 * row + row_bit
                part = carried[row, :, :, row_bit * lanes : (row_bit + 1) * lanes]
                downs[level][spot] = (images[level][spot] + part).astype(BF16)

    down_copy = pltpu.make_async_copy(downs[0], down_hbm, local.at[len(names) + patch // chunk])
    down_copy.start()
    for is_late, numbers in enumerate((early, late)):
        for number in numbers:
            sx, sy = SIDES[number]

            @pl.when(inside(-sx, -sy))
            def _():
                sample_copy(number, is_late).wait_recv()

            @pl.when(jnp.logical_not(inside(-sx, -sy)))
            def _():
                zero_copy(number, is_late).wait()

            @pl.when(inside(sx, sy))
            def _():
                sample_copy(number, is_late).wait_send()

    for number in range(len(SIDES)):

        @pl.when(sends(number))
        def _():
            for level in range(levels):
                halo_copy(level, number).wait_send()

    down_copy.wait()
    for dr, dc in moves:
        top_copy(dr, dc).wait_send()


def finish_kernel(strip, rank, *refs):
    samples_hbm, row_rims, col_rims, near_hbm, down_hbm, basis_hbm, out_hbm = refs[:7]
    samples, near, down, basis, out, rows_sem, out_sem, sems = refs[7:]
    patch, _, vectors, sources = out.shape

    def rows_in(row):
        return pltpu.make_async_copy(
            samples_hbm.at[row], samples.at[row + 1, pl.ds(1, patch)], rows_sem.at[row]
        )

    inner = pl.ds(1, patch)
    fetch = [
        (near_hbm, near),
        (basis_hbm, basis),
        (row_rims.at[0], samples.at[0]),
        (col_rims.at[0], samples.at[inner, pl.ds(0, 1)]),
        (col_rims.at[1], samples.at[inner, pl.ds(patch + 1, 1)]),
        (down_hbm, down),
        (row_rims.at[1], samples.at[patch + 1]),
    ]
    fetch = [pltpu.make_async_copy(*pair, sems.at[n]) for n, pair in enumerate(fetch)]
    for copy in fetch[:5]:
        copy.start()
    for row in range(patch):
        rows_in(row).start()
        if row == strip:
            fetch[5].start()
    fetch[6].start()
    for copy in fetch[:6]:
        copy.wait()
    for row in range(strip):
        rows_in(row).wait()
    basis2 = twice(basis[...])

    def rows_out(number):
        spot = pl.ds(number * strip, strip)
        return pltpu.make_async_copy(out.at[spot], out_hbm.at[spot], out_sem.at[number])

    def body(number, carry):
        begin = number * strip

        @pl.when(begin + strip < patch)
        def _():
            for row in range(strip):
                rows_in(begin + strip + row).wait()

        @pl.when(begin + strip >= patch)
        def _():
            fetch[6].wait()

        left = jnp.concatenate(
            [
                samples[pl.ds(begin + row, strip), col : col + patch].reshape(-1, sources)
                for row in range(3)
                for col in range(3)
            ],
            axis=-1,
        )
        flat = jnp.concatenate([near[tile] for tile in range(9)], axis=-1)
        far = split_columns(down[pl.ds(begin, strip)].reshape(-1, vectors, 2 * rank), rank)
        summed = dot(left, flat, NT) + dot(far, basis2, NN)
        out[pl.ds(begin, strip)] = summed.astype(BF16).reshape(strip, patch, vectors, sources)
        rows_out(number).start()
        return carry

    lax.fori_loop(0, patch // strip, body, 0)

    def end(number, carry):
        rows_out(number).wait()
        return carry

    lax.fori_loop(0, patch // strip, end, 0)


def shards(
    samples,
    leaf_basis,
    transfer,
    coupling,
    near_tiles,
    codes_local,
    counts_local,
    codes_upper,
    counts_upper,
):
    patch, _, vectors, sources = samples.shape
    rank = leaf_basis.shape[0]
    levels = transfer.shape[0] - 1
    lanes = 2 * rank
    across, along = lax.axis_size("gx"), lax.axis_size("gy")
    steps = 1
    while across >> steps >= 2:
        steps += 1
    hbm = pl.BlockSpec(memory_space=pltpu.MemorySpace.HBM)
    slots = codes_local.shape[-1]
    codes = codes_local.reshape(-1, slots)
    listed_counts = counts_local.transpose(0, 2, 1).reshape(-1, patch)
    far_table, upper_table = spread_tables(rank)

    shapes = [(patch >> level, patch >> (level + 1), vectors, lanes) for level in range(levels)]
    down, row_rims, col_rims = pl.pallas_call(
        functools.partial(main_kernel, levels, rank, steps, (across, along)),
        out_shape=[
            jax.ShapeDtypeStruct(shapes[0], BF16),
            jax.ShapeDtypeStruct((2, patch + 2, vectors, sources), BF16),
            jax.ShapeDtypeStruct((2, patch, 1, vectors, sources), BF16),
        ],
        in_specs=[hbm] * 4 + [pl.BlockSpec(memory_space=pltpu.SMEM)] + [hbm] * 5,
        out_specs=[hbm] * 3,
        scratch_shapes=[
            pltpu.VMEM(samples.shape, BF16),
            pltpu.VMEM(codes.shape, jnp.int32),
            pltpu.VMEM(listed_counts.shape, jnp.int32),
            pltpu.VMEM(codes_upper.shape[::-1], jnp.int32),
            pltpu.VMEM(leaf_basis.shape, BF16),
            pltpu.VMEM(transfer.shape, BF16),
            pltpu.VMEM((2, *coupling.shape), BF16),
            pltpu.VMEM(far_table.shape, BF16),
            pltpu.VMEM(upper_table.shape, BF16),
            pltpu.SemaphoreType.DMA((9 + patch // 4,)),
            pltpu.VMEM((4, GROUP, GROUP), F32),
            pltpu.VMEM((GROUP, GROUP), F32),
            pltpu.VMEM((32, 4 * GROUP), F32),
            pltpu.VMEM((4, KEPT, PAIR_COUNT * lanes), F32),
            pltpu.VMEM((8, 36 * rank), F32),
            pltpu.VMEM((across, along, vectors // 2, lanes), BF16),
            pltpu.VMEM((1, patch, vectors, sources), BF16),
            pltpu.SemaphoreType.DMA((levels + 2, len(SIDES))),
            pltpu.SemaphoreType.DMA((levels + 4, len(SIDES))),
            pltpu.SemaphoreType.DMA((across * along,)),
            pltpu.SemaphoreType.DMA((across * along,)),
        ]
        + [pltpu.VMEM((rows + 4, cols + 2, vectors, lanes), BF16) for rows, cols, _, _ in shapes]
        + [pltpu.VMEM((rows // 2, cols + 2, vectors, lanes), BF16) for rows, cols, _, _ in shapes]
        + [pltpu.VMEM(shape, F32) for shape in shapes]
        + [
            pltpu.VMEM(((across >> step) + 4, (along >> (step + 1)) + 2, vectors, lanes), BF16)
            for step in range(steps)
        ]
        + [pltpu.VMEM(shape, BF16) for shape in shapes],
        compiler_params=pltpu.CompilerParams(
            collective_id=0, has_side_effects=True, vmem_limit_bytes=VMEM_LIMIT
        ),
        name="main",
    )(
        samples,
        codes,
        listed_counts,
        codes_upper.T,
        counts_upper,
        leaf_basis,
        transfer,
        coupling,
        jnp.asarray(far_table),
        jnp.asarray(upper_table),
    )
    strip = 2
    return pl.pallas_call(
        functools.partial(finish_kernel, strip, rank),
        out_shape=jax.ShapeDtypeStruct(samples.shape, BF16),
        in_specs=[hbm] * 6,
        out_specs=hbm,
        scratch_shapes=[
            pltpu.VMEM((patch + 2, patch + 2, vectors, sources), BF16),
            pltpu.VMEM(near_tiles.shape, BF16),
            pltpu.VMEM(shapes[0], BF16),
            pltpu.VMEM(leaf_basis.shape, BF16),
            pltpu.VMEM(samples.shape, BF16),
            pltpu.SemaphoreType.DMA((patch,)),
            pltpu.SemaphoreType.DMA((patch // strip,)),
            pltpu.SemaphoreType.DMA((7,)),
        ],
        compiler_params=pltpu.CompilerParams(vmem_limit_bytes=VMEM_LIMIT),
        name="finish",
    )(samples, row_rims, col_rims, near_tiles, down, leaf_basis)


def solution(mesh):
    placed = (
        P("gx", "gy", None, None),
        P(),
        P(),
        P(),
        P(),
        P("gx", "gy", None, None),
        P("gx", "gy", None),
        P(),
        P(),
    )
    return jax.shard_map(
        shards, mesh=mesh, in_specs=placed, out_specs=P("gx", "gy", None, None), check_vma=False
    )
```

```python
import functools

import jax
import jax.numpy as jnp
import numpy as np
from jax import lax
from jax.experimental import pallas as pl
from jax.experimental.pallas import tpu as pltpu
from jax.sharding import PartitionSpec as P

MESH = pl.DeviceIdType.MESH
F32 = jnp.float32
BF16 = jnp.bfloat16
NT = (((1,), (1,)), ((), ()))
NN = (((1,), (0,)), ((), ()))
VMEM_LIMIT = 50 * 1024 * 1024
AXES = ("gx", "gy")
SIDES = [(sx, sy) for sx in (-1, 0, 1) for sy in (-1, 0, 1) if (sx, sy) != (0, 0)]


def dot(a, b, dims):
    return lax.dot_general(a, b, dims, preferred_element_type=F32)


def twice(matrix):
    return jnp.concatenate([matrix, matrix], axis=0)


def low_half(shape, rank):
    return lax.broadcasted_iota(jnp.int32, shape, len(shape) - 1) < rank


def pair_columns(wide, vectors, rank, swap=False):
    pairs = wide.reshape(-1, 2, vectors, 2 * rank)
    even, odd = (pairs[:, 1], pairs[:, 0]) if swap else (pairs[:, 0], pairs[:, 1])
    return jnp.where(low_half(even.shape, rank), even, odd).astype(BF16)


def split_columns(paired, rank):
    count, vectors, lanes = paired.shape
    low = low_half((1, lanes), rank).astype(F32).astype(BF16)
    both = jnp.stack([paired * low, paired * (1 - low)], axis=1)
    return both.reshape(count * 2 * vectors, lanes)


def span(side, size, width):
    if side == 0:
        return pl.ds(0, size), pl.ds(width, size)
    if side > 0:
        return pl.ds(size - width, width), pl.ds(0, width)
    return pl.ds(0, width), pl.ds(width + size, width)


FINISH_LIMIT = 16 * 1024 * 1024
SHARED = 2


def far_pairs(row_bit, col_bit):
    near_rows = [1 + row_bit, 2 + row_bit, 3 + row_bit]
    far_rows = [row for row in range(6) if row not in near_rows]
    full, single = (2, 0) if col_bit == 0 else (0, 2)
    cells = [(row, pair) for row in far_rows for pair in range(3)]
    cells += [(row, full) for row in near_rows]
    entries = [("full", r, p, None, 6 * r + 2 * p, 6 * r + 2 * p + 1) for r, p in cells]
    first, last = [row for row in near_rows if row != SHARED]
    column = 0 if col_bit == 0 else 5
    codes = [6 * first + column, 6 * SHARED + column]
    low, high = codes if col_bit == 0 else codes[::-1]
    entries.append(("both", first, single, SHARED, low, high))
    code = 6 * last + column
    low, high = (code, -1) if col_bit == 0 else (-1, code)
    entries.append(("half", last, single, None, low, high))
    return entries


PARITIES = [(row_bit, col_bit) for row_bit in range(2) for col_bit in range(2)]
PAIRS = {parity: far_pairs(*parity) for parity in PARITIES}
PAIR_COUNT = len(PAIRS[0, 0])
CODE_ROWS = 48
GROUP = 128
KEPT = 96


def spread_tables(rank):
    def table(codes):
        lanes = np.repeat(np.array(codes), rank)
        return (np.arange(CODE_ROWS)[:, None] == lanes[None]).astype(np.float32)

    far = [table([c for e in PAIRS[p] for c in e[4:6]]) for p in PARITIES]
    return np.stack(far).astype(BF16), table(range(36)).astype(BF16)


def main_kernel(levels, rank, steps, counts, *refs):
    (samples_hbm, codes_hbm, counts_hbm, codes_upper_hbm, counts_upper) = refs[:5]
    (basis_hbm, transfer_hbm, coupling_hbm, near_hbm, table_hbm, table_upper_hbm) = refs[5:11]
    near_sum, leaf_down, basis = refs[11:14]
    scratch = refs[14:]
    (samples, codes, listed_counts, codes_upper) = scratch[:4]
    (row_rims, transfer, coupling, near, table, table_upper) = scratch[4:10]
    local, codes_flat, turned_counts, turned, masks, upper_masks = scratch[10:16]
    tops, col_rims, send, recv, top_send, top_recv = scratch[16:22]
    scratch = scratch[22:]
    padded, swapped, images = scratch[:levels], scratch[levels : 2 * levels], scratch[2 * levels : 3 * levels]
    uppers = scratch[3 * levels : 3 * levels + steps]
    downs = (leaf_down, *scratch[3 * levels + steps :])
    patch, _, vectors, sources = samples_hbm.shape
    across, along = counts
    lanes = 2 * rank
    row_index, col_index = lax.axis_index("gx"), lax.axis_index("gy")

    chunk = 4
    fetch = [
        (codes_hbm, codes),
        (counts_hbm, listed_counts),
        (codes_upper_hbm, codes_upper),
        (coupling_hbm, coupling.at[1]),
        (basis_hbm, basis),
        (table_hbm, table),
        (table_upper_hbm, table_upper),
        (transfer_hbm, transfer),
        (near_hbm, near),
    ]
    names = ["codes", "counts", "upper", "coupling", "basis"]
    names += ["table", "table_upper", "transfer", "near"]
    fetch = {
        name: pltpu.make_async_copy(*pair, local.at[number])
        for number, (name, pair) in enumerate(zip(names, fetch))
    }

    def rows_in(number):
        return pltpu.make_async_copy(
            samples_hbm.at[pl.ds(number * chunk, chunk)],
            samples.at[pl.ds(1 + number * chunk, chunk), pl.ds(1, patch)],
            local.at[len(names) + number],
        )

    for name in ("codes", "counts", "upper", "basis"):
        fetch[name].start()
    for number in range(patch // chunk):
        rows_in(number).start()
    for name in ("transfer", "coupling", "table", "table_upper", "near"):
        fetch[name].start()

    def clear_border(target, height, width):
        rows, cols, *tail = target.shape
        for top, tall, left, wide in (
            (0, height, 0, cols),
            (rows - height, height, 0, cols),
            (height, rows - 2 * height, 0, width),
            (height, rows - 2 * height, cols - width, width),
        ):
            target[top : top + tall, left : left + wide] = jnp.zeros((tall, wide, *tail), BF16)

    clear_border(samples, 1, 1)
    row_rims[...] = jnp.zeros(row_rims.shape, BF16)
    col_rims[...] = jnp.zeros(col_rims.shape, BF16)
    for level in range(levels):
        clear_border(padded[level], 2, 1)

    there_rows = [(row_index + step) % across for step in range(across)]
    there_cols = [(col_index + step) % along for step in range(along)]
    moves = [(dr, dc) for dr in range(across) for dc in range(along) if (dr, dc) != (0, 0)]
    barrier = pltpu.get_barrier_semaphore()
    for dr, dc in moves:
        pl.semaphore_signal(
            barrier, inc=1, device_id=(there_rows[dr], there_cols[dc]), device_id_type=MESH
        )

    def top_copy(dr, dc, from_row=None, from_col=None):
        from_row = row_index if from_row is None else from_row
        from_col = col_index if from_col is None else from_col
        return pltpu.make_async_remote_copy(
            src_ref=tops.at[row_index, col_index],
            dst_ref=tops.at[from_row, from_col],
            send_sem=top_send.at[dr * along + dc],
            recv_sem=top_recv.at[dr * along + dc],
            device_id=(there_rows[dr], there_cols[dc]),
            device_id_type=MESH,
        )

    def halo_copy(level, number):
        sx, sy = SIDES[number]
        ref = padded[level]
        rows_from, rows_to = span(sx, patch >> level, 2)
        cols_from, cols_to = span(sy, patch >> (level + 1), 1)
        rows_from = pl.ds(rows_from.start + 2, rows_from.size)
        corner = sx != 0 and sy != 0
        cols_from = cols_to if corner else pl.ds(cols_from.start + 1, cols_from.size)
        return pltpu.make_async_remote_copy(
            src_ref=ref.at[rows_from, cols_from],
            dst_ref=ref.at[rows_to, cols_to],
            send_sem=send.at[level, number],
            recv_sem=recv.at[level, number],
            device_id=(row_index + sx, col_index if corner else col_index + sy),
            device_id_type=MESH,
        )

    def rim_spot(number, late):
        sx, sy = SIDES[number]
        _, cols_to = span(sy, patch, 1)
        if sx == 0:
            return col_rims.at[0 if sy > 0 else 1, pl.ds(1 + late * (patch // 2), patch // 2)]
        return row_rims.at[pl.ds(0 if sx > 0 else 1, 1), cols_to]

    def sample_copy(number, late):
        sx, sy = SIDES[number]
        rows_from, _ = span(sx, patch, 1)
        cols_from, _ = span(sy, patch, 1)
        if sx == 0:
            rows_from = pl.ds(late * (patch // 2), patch // 2)
        return pltpu.make_async_remote_copy(
            src_ref=samples_hbm.at[rows_from, cols_from],
            dst_ref=rim_spot(number, late),
            send_sem=send.at[levels + late, number],
            recv_sem=recv.at[levels + late, number],
            device_id=(row_index + sx, col_index + sy),
            device_id_type=MESH,
        )

    def inside(sx, sy):
        there_row, there_col = row_index + sx, col_index + sy
        return (there_row >= 0) & (there_row < across) & (there_col >= 0) & (there_col < along)

    numbered = list(enumerate(SIDES))
    column_sides = [n for n, (sx, sy) in numbered if sx == 0]
    row_sides = [n for n, (sx, sy) in numbered if sy == 0]
    corners = [n for n, (sx, sy) in numbered if sx != 0 and sy != 0]

    def sends(number):
        sx, sy = SIDES[number]
        return inside(sx, 0) & inside(0, -sy) if number in corners else inside(sx, sy)

    early = column_sides
    late = column_sides + row_sides + corners

    def start_samples(numbers, is_late):
        for number in numbers:

            @pl.when(inside(*SIDES[number]))
            def _():
                sample_copy(number, is_late).start()

    def start_halo(which, numbers):
        for number in numbers:

            @pl.when(sends(number))
            def _():
                for level in which:
                    halo_copy(level, number).start()

    def wait_halo(which, numbers):
        for number in numbers:
            sx, sy = SIDES[number]

            @pl.when(inside(-sx, -sy))
            def _():
                for level in which:
                    halo_copy(level, number).wait_recv()

    fetch["codes"].wait()
    fetch["counts"].wait()
    slots = codes.shape[-1]
    turned_counts[0 : listed_counts.shape[0], 0:patch] = listed_counts[...].astype(F32)
    turned_counts[...] = jnp.transpose(turned_counts[...])
    codes_flat[...] = jnp.full(codes_flat.shape, -1.0, F32)
    slot_lane = lax.broadcasted_iota(jnp.int32, (patch // 2, slots), 1).astype(F32)
    starts = [0]
    for level in range(levels):
        starts.append(starts[-1] + (patch >> (level + 1)) ** 2)
    for level in range(levels):
        size = patch >> level
        half = size // 2
        for row in range(size):
            for bit in range(2):
                begin = ((row << level) * patch + (bit << level)) * levels + level
                if half > 1:
                    listed = codes[pl.ds(begin, half, stride=levels << (level + 1)), :]
                    column = pl.ds(bit << level, half, stride=2 << level)
                else:
                    listed = codes[pl.ds(begin, 1), :]
                    column = pl.ds(bit << level, 1)
                lane = (row << level) * levels + level
                count = turned_counts[column, :][:, lane : lane + 1]
                spot = starts[level] + (row // 2) * half
                codes_flat[row % 2 * 2 + bit, spot : spot + half, 0:slots] = jnp.where(
                    slot_lane[:half] < count, listed.astype(F32), -1.0
                )
    pl.semaphore_wait(barrier, len(moves))
    start_samples(early, 0)

    fetch["basis"].wait()
    own_basis = twice(basis[...])

    def project(number, carry):
        rows_in(number).wait()
        rows = samples[pl.ds(1 + number * chunk, chunk), 1 : 1 + patch].reshape(-1, sources)
        wide = dot(rows, own_basis, NT).reshape(chunk, patch * vectors, lanes)
        for row in range(chunk):
            padded[0][number * chunk + row + 2, 1 : 1 + patch // 2] = pair_columns(
                wide[row], vectors, rank
            )
            if row % 2 == 0:
                swapped[0][number * (chunk // 2) + row // 2, 1 : 1 + patch // 2] = pair_columns(
                    wide[row], vectors, rank, True
                )
        return carry

    lax.fori_loop(0, patch // chunk, project, 0)
    start_halo([0], column_sides + row_sides)
    fetch["transfer"].wait()

    for level in range(levels):
        child = padded[level]
        matrix = twice(transfer[level])
        cols = patch >> (level + 1)
        grouped = jnp.concatenate(
            [
                jnp.concatenate(
                    [child[2 * row + 2, 1 : 1 + cols], child[2 * row + 3, 1 : 1 + cols]], axis=-1
                ).reshape(-1, 4 * rank)
                for row in range(cols)
            ],
            axis=0,
        )
        lifted = dot(grouped, matrix, NT)
        if level < levels - 1:
            lifted = lifted.reshape(cols, cols * vectors, lanes)
            for row in range(cols):
                padded[level + 1][row + 2, 1 : 1 + cols // 2] = pair_columns(
                    lifted[row], vectors, rank
                )
                if row % 2 == 0:
                    swapped[level + 1][row // 2, 1 : 1 + cols // 2] = pair_columns(
                        lifted[row], vectors, rank, True
                    )
        else:
            half = vectors // 2
            tops[row_index, col_index] = jnp.where(
                low_half((half, lanes), rank), lifted[:half], lifted[half:]
            ).astype(BF16)

    start_halo(range(levels - 1, 0, -1), column_sides + row_sides)
    for dr, dc in moves:
        top_copy(dr, dc).start()
    start_samples(late, 1)

    fetch["upper"].wait()
    turns = [jnp.transpose(codes_flat[parity])[0:slots] for parity in range(4)]
    begin = 0
    upper_codes = codes_upper[...].astype(F32)
    upper_lane = lax.broadcasted_iota(jnp.int32, upper_codes.shape, 1)
    slot_row = lax.broadcasted_iota(jnp.int32, (slots, 1), 0)
    group_lane = lax.broadcasted_iota(jnp.int32, (slots, GROUP), 1)
    for step in range(steps):
        cols = along >> step
        index = begin + (row_index // 2**step) * cols + col_index // 2**step
        listed = jnp.sum(jnp.where(upper_lane == index, upper_codes, 0.0), axis=1, keepdims=True)
        listed = jnp.where(slot_row < counts_upper[index], listed, -1.0)
        turns[0] = jnp.where(group_lane == KEPT - 8 + step, listed, turns[0])
        begin += (across >> step) * cols
    for parity in range(4):
        turned[0:slots, parity * GROUP : (parity + 1) * GROUP] = turns[parity]
    code = lax.broadcasted_iota(jnp.int32, (CODE_ROWS, GROUP), 0).astype(F32)
    founds = []
    for parity in range(4):
        found = jnp.zeros((GROUP, GROUP), F32)[0:CODE_ROWS]
        for slot in range(slots):
            listed = turned[slot : slot + 1, parity * GROUP : (parity + 1) * GROUP]
            found = jnp.where(code == listed, 1.0, found)
        found = jnp.concatenate([found, jnp.zeros((GROUP - CODE_ROWS, GROUP), F32)], axis=0)
        founds.append(jnp.transpose(found)[0:KEPT, 0:CODE_ROWS].astype(BF16))
    fetch["coupling"].wait()

    def shift(level, carry):
        for part in range(coupling.shape[2]):
            coupling[0, level, part, :, 0 : 6 * rank] = coupling[1, level, part, :, rank : 7 * rank]
        return carry

    lax.fori_loop(0, coupling.shape[1], shift, 0)
    fetch["table"].wait()
    fetch["table_upper"].wait()
    for parity in range(4):
        masks[parity] = dot(founds[parity], table[parity], NN)
    upper_masks[...] = dot(founds[0][KEPT - 16 :], table_upper[...], NN)[8:]

    low_lanes = low_half((1, lanes), rank).astype(F32).astype(BF16)
    high_lanes = 1 - low_lanes

    def weights(level, row_bit):
        sides = []
        for col_bit in range(2):
            parts = []
            for kind, row, pair, other, _, _ in PAIRS[row_bit, col_bit]:
                spot = pl.ds(pair * lanes, lanes)
                part = coupling[col_bit, level, row + 1 - row_bit, :, spot]
                if kind == "both":
                    second = coupling[1 - col_bit, level, other + 1 - row_bit, :, spot]
                    if col_bit == 0:
                        part = part * low_lanes + second * high_lanes
                    else:
                        part = part * high_lanes + second * low_lanes
                parts.append(part)
            parts = jnp.concatenate(parts, axis=-1)
            blank = jnp.zeros_like(parts)
            sides.append(jnp.concatenate([parts, blank] if col_bit == 0 else [blank, parts], axis=0))
        return jnp.concatenate(sides, axis=-1)

    def couple(level, cells):
        cols = patch >> (level + 1)
        for row_bit in range(2):
            left = []
            for row, col in cells:
                line = []
                for col_bit in range(2):
                    spot = starts[level] + row * cols + col
                    mask = masks[row_bit * 2 + col_bit, pl.ds(spot, 1), :]
                    mask = jnp.broadcast_to(mask, (16, PAIR_COUNT * lanes)).astype(BF16)
                    parts = []
                    for kind, part_row, pair, _, _, _ in PAIRS[row_bit, col_bit]:
                        part = padded[level][2 * row + part_row, col + pair]
                        if kind == "both":
                            second = swapped[level][row, col + pair]
                            if col_bit == 0:
                                part = part * low_lanes + second * high_lanes
                            else:
                                part = part * high_lanes + second * low_lanes
                        parts.append(part)
                    parts = jnp.concatenate(parts, axis=-1)
                    parts = parts.reshape(-1, 16, PAIR_COUNT * lanes) * mask[None]
                    line.append(parts.reshape(vectors, PAIR_COUNT * lanes))
                left.append(jnp.concatenate(line, axis=-1))
            image = dot(jnp.concatenate(left, axis=0), weights(level, row_bit), NT)
            image = image.reshape(len(cells), vectors, lanes)
            for number, (row, col) in enumerate(cells):
                images[level][2 * row + row_bit, col] = image[number]

    inner = range(1, patch // 2 - 1)

    def inner_rows(pair, carry):
        couple(0, [(1 + 2 * pair + step, col) for step in range(2) for col in inner])
        return carry

    lax.fori_loop(0, len(inner) // 2, inner_rows, 0)

    last = patch // 2 - 1
    own = range(levels)
    wait_halo([0], row_sides)
    couple(0, [(row, col) for row in (0, last) for col in inner])
    fetch["near"].wait()
    strip = 2

    def near_body(number, carry):
        spot = pl.ds(number * strip, strip)
        left = jnp.concatenate(
            [
                samples[pl.ds(number * strip + row, strip), col : col + patch].reshape(-1, sources)
                for row in range(3)
                for col in range(3)
            ],
            axis=-1,
        )
        flat = jnp.concatenate([near[tile] for tile in range(9)], axis=-1)
        near_sum[spot] = dot(left, flat, NT).reshape(strip, patch * vectors, sources)
        return carry

    lax.fori_loop(0, patch // strip - 2, near_body, 0)
    wait_halo(own, column_sides)
    start_halo(own, corners)
    lax.fori_loop(patch // strip - 2, patch // strip, near_body, 0)
    for level in range(levels):
        rows, cols = patch >> (level + 1), (patch >> (level + 1)) + 2
        for edge in (0, cols - 1):
            for row in range(rows):
                piece = padded[level][2 * row + 2, edge].astype(F32)
                swapped[level][row, edge] = pltpu.roll(piece, rank, 1).astype(BF16)

    wait_halo(range(1, levels), row_sides)
    wait_halo(own, corners)
    couple(0, [(row, col) for row in range(patch // 2) for col in (0, last)])
    for level in range(1, levels):
        size = patch >> (level + 1)
        couple(level, [(row, col) for row in range(size) for col in range(size)])

    for dr, dc in moves:
        top_copy(dr, dc, (row_index - dr) % across, (col_index - dc) % along).wait_recv()

    def window(ref, row, col):
        return jnp.concatenate(
            [ref[row + code, col + step] for code in range(6) for step in range(3)], axis=-1
        )

    uppers[0][...] = jnp.zeros(uppers[0].shape, BF16)
    for row in range(across):
        for col in range(along // 2):
            even, odd = (tops[row, 2 * col + bit].astype(F32) for bit in range(2))
            low = low_half(even.shape, rank)
            first = jnp.where(low, even, pltpu.roll(odd, rank, 1))
            second = jnp.where(low, pltpu.roll(even, rank, 1), odd)
            both = jnp.concatenate([first, second], axis=0)
            uppers[0][row + 2, col + 1] = both.astype(BF16)
    top_matrix = twice(transfer[levels])
    for step in range(steps - 1):
        child, parent = uppers[step], uppers[step + 1]
        parent[...] = jnp.zeros(parent.shape, BF16)
        rows, cols = across >> step, along >> (step + 1)
        grouped = jnp.concatenate(
            [
                jnp.concatenate(
                    [child[2 * row + 2, 1 : 1 + cols], child[2 * row + 3, 1 : 1 + cols]], axis=-1
                ).reshape(-1, 4 * rank)
                for row in range(rows // 2)
            ],
            axis=0,
        )
        lifted = dot(grouped, top_matrix, NT).reshape(rows // 2, cols * vectors, lanes)
        for row in range(rows // 2):
            parent[row + 2, 1 : 1 + cols // 2] = pair_columns(lifted[row], vectors, rank)
    low = low_half((vectors, lanes), rank)
    upper_images = []
    for step in range(steps):
        row, col = row_index // 2**step, col_index // 2**step
        slab = window(uppers[step], 2 * (row // 2), col // 2)
        mask = jnp.broadcast_to(upper_masks[step : step + 1, :], (16, 36 * rank)).astype(BF16)
        slab = (slab.reshape(-1, 16, 36 * rank) * mask[None]).reshape(slab.shape)
        flat = jnp.concatenate(
            [coupling[col % 2, levels, code + 1 - row % 2, :, 0 : 6 * rank] for code in range(6)],
            axis=-1,
        )
        upper_images.append(dot(slab, twice(flat), NT))
    down = upper_images[-1]
    for step in range(steps - 2, -1, -1):
        row, col = row_index // 2**step, col_index // 2**step
        carried = dot(down.astype(BF16) * low_lanes, top_matrix, NN)
        part = jnp.where(row % 2 == 0, carried[:, :lanes], carried[:, lanes:])
        part = jnp.where(low == (col % 2 == 0), part, pltpu.roll(part, rank, 1))
        down = upper_images[step] + part

    for level in range(levels - 1, -1, -1):
        size = patch >> (level + 1)
        if level == levels - 1:
            parent = down.astype(BF16) * low_lanes
        else:
            parent = jnp.concatenate(
                [split_columns(downs[level + 1][row], rank) for row in range(size)], axis=0
            )
        carried = dot(parent, twice(transfer[level]), NN)
        carried = carried.reshape(size, size, vectors, 2 * lanes)
        for row in range(size):
            for row_bit in range(2):
                spot = 2 * row + row_bit
                part = carried[row, :, :, row_bit * lanes : (row_bit + 1) * lanes]
                downs[level][spot] = (images[level][spot] + part).astype(BF16)

    for is_late, numbers in enumerate((early, late)):
        for number in numbers:
            sx, sy = SIDES[number]

            @pl.when(inside(-sx, -sy))
            def _():
                sample_copy(number, is_late).wait_recv()

            @pl.when(inside(sx, sy))
            def _():
                sample_copy(number, is_late).wait_send()

    for side, column, step in ((0, 0, 0), (1, patch - 1, 2)):
        left = jnp.concatenate(
            [col_rims[side, part : part + patch, 0].reshape(-1, sources) for part in range(3)],
            axis=-1,
        )
        flat = jnp.concatenate([near[3 * part + step] for part in range(3)], axis=-1)
        spot = pl.ds(column * vectors, vectors)
        extra = dot(left, flat, NT).reshape(patch, vectors, sources)
        near_sum[:, spot, :] = near_sum[:, spot, :] + extra
    for side, row, step in ((0, 0, 0), (1, patch - 1, 6)):
        left = jnp.concatenate(
            [row_rims[side, part : part + patch].reshape(-1, sources) for part in range(3)],
            axis=-1,
        )
        flat = jnp.concatenate([near[step + part] for part in range(3)], axis=-1)
        near_sum[row] = near_sum[row] + dot(left, flat, NT)

    for number in range(len(SIDES)):

        @pl.when(sends(number))
        def _():
            for level in range(levels):
                halo_copy(level, number).wait_send()

    for dr, dc in moves:
        top_copy(dr, dc).wait_send()


def finish_kernel(rank, near_sum, down, basis, out_hbm, out, sems):
    patch, _, vectors, sources = out.shape
    chunks = sems.shape[0]
    rows = patch // chunks
    basis2 = twice(basis[...])

    def rows_out(number):
        spot = pl.ds(number * rows, rows)
        return pltpu.make_async_copy(out.at[spot], out_hbm.at[spot], sems.at[number])

    def body(number, carry):
        spot = pl.ds(number * rows, rows)
        far = split_columns(down[spot].reshape(-1, vectors, 2 * rank), rank)
        summed = near_sum[spot].reshape(-1, sources) + dot(far, basis2, NN)
        out[spot] = summed.astype(BF16).reshape(rows, patch, vectors, sources)
        rows_out(number).start()
        return carry

    lax.fori_loop(0, chunks, body, 0)

    def end(number, carry):
        rows_out(number).wait()
        return carry

    lax.fori_loop(0, chunks, end, 0)


def shards(
    samples,
    leaf_basis,
    transfer,
    coupling,
    near_tiles,
    codes_local,
    counts_local,
    codes_upper,
    counts_upper,
):
    patch, _, vectors, sources = samples.shape
    rank = leaf_basis.shape[0]
    levels = transfer.shape[0] - 1
    lanes = 2 * rank
    across, along = lax.axis_size("gx"), lax.axis_size("gy")
    steps = 1
    while across >> steps >= 2:
        steps += 1
    hbm = pl.BlockSpec(memory_space=pltpu.MemorySpace.HBM)
    vmem = pl.BlockSpec(memory_space=pltpu.VMEM)
    slots = codes_local.shape[-1]
    codes = codes_local.reshape(-1, slots)
    listed_counts = counts_local.transpose(0, 2, 1).reshape(-1, patch)
    far_table, upper_table = spread_tables(rank)

    shapes = [(patch >> level, patch >> (level + 1), vectors, lanes) for level in range(levels)]
    near_sum, down, basis = pl.pallas_call(
        functools.partial(main_kernel, levels, rank, steps, (across, along)),
        out_shape=[
            pltpu.VMEM((patch, patch * vectors, sources), F32),
            pltpu.VMEM(shapes[0], BF16),
            pltpu.VMEM(leaf_basis.shape, BF16),
        ],
        in_specs=[hbm] * 4 + [pl.BlockSpec(memory_space=pltpu.SMEM)] + [hbm] * 6,
        out_specs=[vmem] * 3,
        scratch_shapes=[
            pltpu.VMEM((patch + 2, patch + 2, vectors, sources), BF16),
            pltpu.VMEM(codes.shape, jnp.int32),
            pltpu.VMEM(listed_counts.shape, jnp.int32),
            pltpu.VMEM(codes_upper.shape[::-1], jnp.int32),
            pltpu.VMEM((2, patch + 2, vectors, sources), BF16),
            pltpu.VMEM(transfer.shape, BF16),
            pltpu.VMEM((2, *coupling.shape), BF16),
            pltpu.VMEM(near_tiles.shape, BF16),
            pltpu.VMEM(far_table.shape, BF16),
            pltpu.VMEM(upper_table.shape, BF16),
            pltpu.SemaphoreType.DMA((9 + patch // 4,)),
            pltpu.VMEM((4, GROUP, GROUP), F32),
            pltpu.VMEM((GROUP, GROUP), F32),
            pltpu.VMEM((32, 4 * GROUP), F32),
            pltpu.VMEM((4, KEPT, PAIR_COUNT * lanes), F32),
            pltpu.VMEM((8, 36 * rank), F32),
            pltpu.VMEM((across, along, vectors // 2, lanes), BF16),
            pltpu.VMEM((2, patch + 2, 1, vectors, sources), BF16),
            pltpu.SemaphoreType.DMA((levels + 2, len(SIDES))),
            pltpu.SemaphoreType.DMA((levels + 2, len(SIDES))),
            pltpu.SemaphoreType.DMA((across * along,)),
            pltpu.SemaphoreType.DMA((across * along,)),
        ]
        + [pltpu.VMEM((rows + 4, cols + 2, vectors, lanes), BF16) for rows, cols, _, _ in shapes]
        + [pltpu.VMEM((rows // 2, cols + 2, vectors, lanes), BF16) for rows, cols, _, _ in shapes]
        + [pltpu.VMEM(shape, F32) for shape in shapes]
        + [
            pltpu.VMEM(((across >> step) + 4, (along >> (step + 1)) + 2, vectors, lanes), BF16)
            for step in range(steps)
        ]
        + [pltpu.VMEM(shape, BF16) for shape in shapes[1:]],
        compiler_params=pltpu.CompilerParams(
            collective_id=0, has_side_effects=True, vmem_limit_bytes=VMEM_LIMIT
        ),
        name="main",
    )(
        samples,
        codes,
        listed_counts,
        codes_upper.T,
        counts_upper,
        leaf_basis,
        transfer,
        coupling,
        near_tiles,
        jnp.asarray(far_table),
        jnp.asarray(upper_table),
    )
    return pl.pallas_call(
        functools.partial(finish_kernel, rank),
        out_shape=jax.ShapeDtypeStruct(samples.shape, BF16),
        in_specs=[vmem] * 3,
        out_specs=hbm,
        scratch_shapes=[
            pltpu.VMEM(samples.shape, BF16),
            pltpu.SemaphoreType.DMA((patch // 2,)),
        ],
        compiler_params=pltpu.CompilerParams(vmem_limit_bytes=FINISH_LIMIT),
        name="finish",
    )(near_sum, down, basis)


def solution(mesh):
    placed = (
        P("gx", "gy", None, None),
        P(),
        P(),
        P(),
        P(),
        P("gx", "gy", None, None),
        P("gx", "gy", None),
        P(),
        P(),
    )
    return jax.shard_map(
        shards, mesh=mesh, in_specs=placed, out_specs=P("gx", "gy", None, None), check_vma=False
    )
```

```python
import functools

import jax
import jax.numpy as jnp
import numpy as np
from jax import lax
from jax.experimental import pallas as pl
from jax.experimental.pallas import tpu as pltpu
from jax.sharding import PartitionSpec as P

MESH = pl.DeviceIdType.MESH
F32 = jnp.float32
BF16 = jnp.bfloat16
NT = (((1,), (1,)), ((), ()))
NN = (((1,), (0,)), ((), ()))
VMEM_LIMIT = 50 * 1024 * 1024
AXES = ("gx", "gy")
SIDES = [(sx, sy) for sx in (-1, 0, 1) for sy in (-1, 0, 1) if (sx, sy) != (0, 0)]


def dot(a, b, dims):
    return lax.dot_general(a, b, dims, preferred_element_type=F32)


def twice(matrix):
    return jnp.concatenate([matrix, matrix], axis=0)


def low_half(shape, rank):
    return lax.broadcasted_iota(jnp.int32, shape, len(shape) - 1) < rank


def pair_columns(wide, vectors, rank, swap=False):
    pairs = wide.reshape(-1, 2, vectors, 2 * rank)
    even, odd = (pairs[:, 1], pairs[:, 0]) if swap else (pairs[:, 0], pairs[:, 1])
    return jnp.where(low_half(even.shape, rank), even, odd).astype(BF16)


def split_columns(paired, rank):
    count, vectors, lanes = paired.shape
    low = low_half((1, lanes), rank).astype(F32).astype(BF16)
    both = jnp.stack([paired * low, paired * (1 - low)], axis=1)
    return both.reshape(count * 2 * vectors, lanes)


def span(side, size, width):
    if side == 0:
        return pl.ds(0, size), pl.ds(width, size)
    if side > 0:
        return pl.ds(size - width, width), pl.ds(0, width)
    return pl.ds(0, width), pl.ds(width + size, width)


FINISH_LIMIT = 16 * 1024 * 1024
SHARED = 2


def far_pairs(row_bit, col_bit):
    near_rows = [1 + row_bit, 2 + row_bit, 3 + row_bit]
    far_rows = [row for row in range(6) if row not in near_rows]
    full, single = (2, 0) if col_bit == 0 else (0, 2)
    cells = [(row, pair) for row in far_rows for pair in range(3)]
    cells += [(row, full) for row in near_rows]
    entries = [("full", r, p, None, 6 * r + 2 * p, 6 * r + 2 * p + 1) for r, p in cells]
    first, last = [row for row in near_rows if row != SHARED]
    column = 0 if col_bit == 0 else 5
    codes = [6 * first + column, 6 * SHARED + column]
    low, high = codes if col_bit == 0 else codes[::-1]
    entries.append(("both", first, single, SHARED, low, high))
    code = 6 * last + column
    low, high = (code, -1) if col_bit == 0 else (-1, code)
    entries.append(("half", last, single, None, low, high))
    return entries


PARITIES = [(row_bit, col_bit) for row_bit in range(2) for col_bit in range(2)]
PAIRS = {parity: far_pairs(*parity) for parity in PARITIES}
PAIR_COUNT = len(PAIRS[0, 0])
CODE_ROWS = 48
GROUP = 128
KEPT = 96


def spread_tables(rank):
    def table(codes):
        lanes = np.repeat(np.array(codes), rank)
        return (np.arange(CODE_ROWS)[:, None] == lanes[None]).astype(np.float32)

    far = [table([c for e in PAIRS[p] for c in e[4:6]]) for p in PARITIES]
    return np.stack(far).astype(BF16), table(range(36)).astype(BF16)


def main_kernel(levels, rank, steps, counts, *refs):
    (samples_hbm, codes_hbm, counts_hbm, codes_upper_hbm, counts_upper) = refs[:5]
    (basis_hbm, transfer_hbm, coupling_hbm, near_hbm, table_hbm, table_upper_hbm) = refs[5:11]
    near_sum, leaf_down, basis = refs[11:14]
    scratch = refs[14:]
    (samples, codes, listed_counts, codes_upper) = scratch[:4]
    (row_rims, transfer, coupling, near, table, table_upper) = scratch[4:10]
    local, codes_flat, turned_counts, turned, masks, upper_masks = scratch[10:16]
    tops, col_rims, send, recv, top_send, top_recv = scratch[16:22]
    scratch = scratch[22:]
    padded, swapped, images = scratch[:levels], scratch[levels : 2 * levels], scratch[2 * levels : 3 * levels]
    uppers = scratch[3 * levels : 3 * levels + steps]
    downs = (leaf_down, *scratch[3 * levels + steps :])
    patch, _, vectors, sources = samples_hbm.shape
    across, along = counts
    lanes = 2 * rank
    row_index, col_index = lax.axis_index("gx"), lax.axis_index("gy")

    chunk = 4
    fetch = [
        (codes_hbm, codes),
        (counts_hbm, listed_counts),
        (codes_upper_hbm, codes_upper),
        (coupling_hbm, coupling.at[1]),
        (basis_hbm, basis),
        (table_hbm, table),
        (table_upper_hbm, table_upper),
        (transfer_hbm, transfer),
        (near_hbm, near),
    ]
    names = ["codes", "counts", "upper", "coupling", "basis"]
    names += ["table", "table_upper", "transfer", "near"]
    fetch = {
        name: pltpu.make_async_copy(*pair, local.at[number])
        for number, (name, pair) in enumerate(zip(names, fetch))
    }

    def rows_in(number):
        return pltpu.make_async_copy(
            samples_hbm.at[pl.ds(number * chunk, chunk)],
            samples.at[pl.ds(1 + number * chunk, chunk), pl.ds(1, patch)],
            local.at[len(names) + number],
        )

    for name in ("codes", "counts", "upper", "table", "table_upper", "basis"):
        fetch[name].start()
    for number in range(patch // chunk):
        rows_in(number).start()
    for name in ("transfer", "coupling", "near"):
        fetch[name].start()

    def clear_border(target, height, width):
        rows, cols, *tail = target.shape
        for top, tall, left, wide in (
            (0, height, 0, cols),
            (rows - height, height, 0, cols),
            (height, rows - 2 * height, 0, width),
            (height, rows - 2 * height, cols - width, width),
        ):
            target[top : top + tall, left : left + wide] = jnp.zeros((tall, wide, *tail), BF16)

    clear_border(samples, 1, 1)
    row_rims[...] = jnp.zeros(row_rims.shape, BF16)
    col_rims[...] = jnp.zeros(col_rims.shape, BF16)
    for level in range(levels):
        clear_border(padded[level], 2, 1)

    there_rows = [(row_index + step) % across for step in range(across)]
    there_cols = [(col_index + step) % along for step in range(along)]
    moves = [(dr, dc) for dr in range(across) for dc in range(along) if (dr, dc) != (0, 0)]
    barrier = pltpu.get_barrier_semaphore()
    for dr, dc in moves:
        pl.semaphore_signal(
            barrier, inc=1, device_id=(there_rows[dr], there_cols[dc]), device_id_type=MESH
        )

    def top_copy(dr, dc, from_row=None, from_col=None):
        from_row = row_index if from_row is None else from_row
        from_col = col_index if from_col is None else from_col
        return pltpu.make_async_remote_copy(
            src_ref=tops.at[row_index, col_index],
            dst_ref=tops.at[from_row, from_col],
            send_sem=top_send.at[dr * along + dc],
            recv_sem=top_recv.at[dr * along + dc],
            device_id=(there_rows[dr], there_cols[dc]),
            device_id_type=MESH,
        )

    def halo_copy(level, number):
        sx, sy = SIDES[number]
        ref = padded[level]
        rows_from, rows_to = span(sx, patch >> level, 2)
        cols_from, cols_to = span(sy, patch >> (level + 1), 1)
        rows_from = pl.ds(rows_from.start + 2, rows_from.size)
        corner = sx != 0 and sy != 0
        cols_from = cols_to if corner else pl.ds(cols_from.start + 1, cols_from.size)
        return pltpu.make_async_remote_copy(
            src_ref=ref.at[rows_from, cols_from],
            dst_ref=ref.at[rows_to, cols_to],
            send_sem=send.at[level, number],
            recv_sem=recv.at[level, number],
            device_id=(row_index + sx, col_index if corner else col_index + sy),
            device_id_type=MESH,
        )

    def rim_spot(number, late):
        sx, sy = SIDES[number]
        _, cols_to = span(sy, patch, 1)
        if sx == 0:
            return col_rims.at[0 if sy > 0 else 1, pl.ds(1 + late * (patch // 2), patch // 2)]
        return row_rims.at[pl.ds(0 if sx > 0 else 1, 1), cols_to]

    def sample_copy(number, late):
        sx, sy = SIDES[number]
        rows_from, _ = span(sx, patch, 1)
        cols_from, _ = span(sy, patch, 1)
        if sx == 0:
            rows_from = pl.ds(late * (patch // 2), patch // 2)
        return pltpu.make_async_remote_copy(
            src_ref=samples_hbm.at[rows_from, cols_from],
            dst_ref=rim_spot(number, late),
            send_sem=send.at[levels + late, number],
            recv_sem=recv.at[levels + late, number],
            device_id=(row_index + sx, col_index + sy),
            device_id_type=MESH,
        )

    def inside(sx, sy):
        there_row, there_col = row_index + sx, col_index + sy
        return (there_row >= 0) & (there_row < across) & (there_col >= 0) & (there_col < along)

    numbered = list(enumerate(SIDES))
    column_sides = [n for n, (sx, sy) in numbered if sx == 0]
    row_sides = [n for n, (sx, sy) in numbered if sy == 0]
    corners = [n for n, (sx, sy) in numbered if sx != 0 and sy != 0]

    def sends(number):
        sx, sy = SIDES[number]
        return inside(sx, 0) & inside(0, -sy) if number in corners else inside(sx, sy)

    early = column_sides
    late = column_sides + row_sides + corners

    def start_samples(numbers, is_late):
        for number in numbers:

            @pl.when(inside(*SIDES[number]))
            def _():
                sample_copy(number, is_late).start()

    def start_halo(which, numbers):
        for number in numbers:

            @pl.when(sends(number))
            def _():
                for level in which:
                    halo_copy(level, number).start()

    def wait_halo(which, numbers):
        for number in numbers:
            sx, sy = SIDES[number]

            @pl.when(inside(-sx, -sy))
            def _():
                for level in which:
                    halo_copy(level, number).wait_recv()

    fetch["codes"].wait()
    fetch["counts"].wait()
    slots = codes.shape[-1]
    turned_counts[0 : listed_counts.shape[0], 0:patch] = listed_counts[...].astype(F32)
    turned_counts[...] = jnp.transpose(turned_counts[...])
    codes_flat[...] = jnp.full(codes_flat.shape, -1.0, F32)
    slot_lane = lax.broadcasted_iota(jnp.int32, (patch // 2, slots), 1).astype(F32)
    starts = [0]
    for level in range(levels):
        starts.append(starts[-1] + (patch >> (level + 1)) ** 2)
    for level in range(levels):
        size = patch >> level
        half = size // 2
        for row in range(size):
            for bit in range(2):
                begin = ((row << level) * patch + (bit << level)) * levels + level
                if half > 1:
                    listed = codes[pl.ds(begin, half, stride=levels << (level + 1)), :]
                    column = pl.ds(bit << level, half, stride=2 << level)
                else:
                    listed = codes[pl.ds(begin, 1), :]
                    column = pl.ds(bit << level, 1)
                lane = (row << level) * levels + level
                count = turned_counts[column, :][:, lane : lane + 1]
                spot = starts[level] + (row // 2) * half
                codes_flat[row % 2 * 2 + bit, spot : spot + half, 0:slots] = jnp.where(
                    slot_lane[:half] < count, listed.astype(F32), -1.0
                )
    fetch["upper"].wait()
    turns = [jnp.transpose(codes_flat[parity])[0:slots] for parity in range(4)]
    begin = 0
    upper_codes = codes_upper[...].astype(F32)
    upper_lane = lax.broadcasted_iota(jnp.int32, upper_codes.shape, 1)
    slot_row = lax.broadcasted_iota(jnp.int32, (slots, 1), 0)
    group_lane = lax.broadcasted_iota(jnp.int32, (slots, GROUP), 1)
    for step in range(steps):
        cols = along >> step
        index = begin + (row_index // 2**step) * cols + col_index // 2**step
        listed = jnp.sum(jnp.where(upper_lane == index, upper_codes, 0.0), axis=1, keepdims=True)
        listed = jnp.where(slot_row < counts_upper[index], listed, -1.0)
        turns[0] = jnp.where(group_lane == KEPT - 8 + step, listed, turns[0])
        begin += (across >> step) * cols
    for parity in range(4):
        turned[0:slots, parity * GROUP : (parity + 1) * GROUP] = turns[parity]
    code = lax.broadcasted_iota(jnp.int32, (CODE_ROWS, GROUP), 0).astype(F32)
    founds = []
    for parity in range(4):
        found = jnp.zeros((GROUP, GROUP), F32)[0:CODE_ROWS]
        for slot in range(slots):
            listed = turned[slot : slot + 1, parity * GROUP : (parity + 1) * GROUP]
            found = jnp.where(code == listed, 1.0, found)
        found = jnp.concatenate([found, jnp.zeros((GROUP - CODE_ROWS, GROUP), F32)], axis=0)
        founds.append(jnp.transpose(found)[0:KEPT, 0:CODE_ROWS].astype(BF16))
    fetch["table"].wait()
    fetch["table_upper"].wait()
    for parity in range(4):
        masks[parity] = dot(founds[parity], table[parity], NN)
    upper_masks[...] = dot(founds[0][KEPT - 16 :], table_upper[...], NN)[8:]

    pl.semaphore_wait(barrier, len(moves))

    fetch["basis"].wait()
    own_basis = twice(basis[...])

    def project(number, carry):
        rows_in(number).wait()
        rows = samples[pl.ds(1 + number * chunk, chunk), 1 : 1 + patch].reshape(-1, sources)
        wide = dot(rows, own_basis, NT).reshape(chunk, patch * vectors, lanes)
        for row in range(chunk):
            padded[0][number * chunk + row + 2, 1 : 1 + patch // 2] = pair_columns(
                wide[row], vectors, rank
            )
            if row % 2 == 0:
                swapped[0][number * (chunk // 2) + row // 2, 1 : 1 + patch // 2] = pair_columns(
                    wide[row], vectors, rank, True
                )
        return carry

    lax.fori_loop(0, patch // chunk, project, 0)
    start_halo([0], column_sides + row_sides)
    fetch["transfer"].wait()

    for level in range(levels):
        child = padded[level]
        matrix = twice(transfer[level])
        cols = patch >> (level + 1)
        grouped = jnp.concatenate(
            [
                jnp.concatenate(
                    [child[2 * row + 2, 1 : 1 + cols], child[2 * row + 3, 1 : 1 + cols]], axis=-1
                ).reshape(-1, 4 * rank)
                for row in range(cols)
            ],
            axis=0,
        )
        lifted = dot(grouped, matrix, NT)
        if level < levels - 1:
            lifted = lifted.reshape(cols, cols * vectors, lanes)
            for row in range(cols):
                padded[level + 1][row + 2, 1 : 1 + cols // 2] = pair_columns(
                    lifted[row], vectors, rank
                )
                if row % 2 == 0:
                    swapped[level + 1][row // 2, 1 : 1 + cols // 2] = pair_columns(
                        lifted[row], vectors, rank, True
                    )
        else:
            half = vectors // 2
            tops[row_index, col_index] = jnp.where(
                low_half((half, lanes), rank), lifted[:half], lifted[half:]
            ).astype(BF16)

    start_halo(range(levels - 1, 0, -1), column_sides + row_sides)
    for dr, dc in moves:
        top_copy(dr, dc).start()
    start_samples(early, 0)
    start_samples(late, 1)

    fetch["coupling"].wait()

    def shift(level, carry):
        for part in range(coupling.shape[2]):
            coupling[0, level, part, :, 0 : 6 * rank] = coupling[1, level, part, :, rank : 7 * rank]
        return carry

    lax.fori_loop(0, coupling.shape[1], shift, 0)
    low_lanes = low_half((1, lanes), rank).astype(F32).astype(BF16)
    high_lanes = 1 - low_lanes

    def weights(level, row_bit):
        sides = []
        for col_bit in range(2):
            parts = []
            for kind, row, pair, other, _, _ in PAIRS[row_bit, col_bit]:
                spot = pl.ds(pair * lanes, lanes)
                part = coupling[col_bit, level, row + 1 - row_bit, :, spot]
                if kind == "both":
                    second = coupling[1 - col_bit, level, other + 1 - row_bit, :, spot]
                    if col_bit == 0:
                        part = part * low_lanes + second * high_lanes
                    else:
                        part = part * high_lanes + second * low_lanes
                parts.append(part)
            parts = jnp.concatenate(parts, axis=-1)
            blank = jnp.zeros_like(parts)
            sides.append(jnp.concatenate([parts, blank] if col_bit == 0 else [blank, parts], axis=0))
        return jnp.concatenate(sides, axis=-1)

    def couple(level, cells):
        cols = patch >> (level + 1)
        for row_bit in range(2):
            left = []
            for row, col in cells:
                line = []
                for col_bit in range(2):
                    spot = starts[level] + row * cols + col
                    mask = masks[row_bit * 2 + col_bit, pl.ds(spot, 1), :]
                    mask = jnp.broadcast_to(mask, (16, PAIR_COUNT * lanes)).astype(BF16)
                    parts = []
                    for kind, part_row, pair, _, _, _ in PAIRS[row_bit, col_bit]:
                        part = padded[level][2 * row + part_row, col + pair]
                        if kind == "both":
                            second = swapped[level][row, col + pair]
                            if col_bit == 0:
                                part = part * low_lanes + second * high_lanes
                            else:
                                part = part * high_lanes + second * low_lanes
                        parts.append(part)
                    parts = jnp.concatenate(parts, axis=-1)
                    parts = parts.reshape(-1, 16, PAIR_COUNT * lanes) * mask[None]
                    line.append(parts.reshape(vectors, PAIR_COUNT * lanes))
                left.append(jnp.concatenate(line, axis=-1))
            image = dot(jnp.concatenate(left, axis=0), weights(level, row_bit), NT)
            image = image.reshape(len(cells), vectors, lanes)
            for number, (row, col) in enumerate(cells):
                images[level][2 * row + row_bit, col] = image[number]

    inner = range(1, patch // 2 - 1)

    def inner_rows(pair, carry):
        couple(0, [(1 + 2 * pair + step, col) for step in range(2) for col in inner])
        return carry

    lax.fori_loop(0, len(inner) // 2, inner_rows, 0)

    last = patch // 2 - 1
    own = range(levels)
    wait_halo([0], row_sides)
    couple(0, [(row, col) for row in (0, last) for col in inner])
    fetch["near"].wait()
    strip = 2

    def near_body(number, carry):
        spot = pl.ds(number * strip, strip)
        left = jnp.concatenate(
            [
                samples[pl.ds(number * strip + row, strip), col : col + patch].reshape(-1, sources)
                for row in range(3)
                for col in range(3)
            ],
            axis=-1,
        )
        flat = jnp.concatenate([near[tile] for tile in range(9)], axis=-1)
        near_sum[spot] = dot(left, flat, NT).reshape(strip, patch * vectors, sources)
        return carry

    lax.fori_loop(0, patch // strip - 2, near_body, 0)
    wait_halo(own, column_sides)
    start_halo(own, corners)
    lax.fori_loop(patch // strip - 2, patch // strip, near_body, 0)
    for level in range(levels):
        rows, cols = patch >> (level + 1), (patch >> (level + 1)) + 2
        for edge in (0, cols - 1):
            for row in range(rows):
                piece = padded[level][2 * row + 2, edge].astype(F32)
                swapped[level][row, edge] = pltpu.roll(piece, rank, 1).astype(BF16)

    wait_halo(range(1, levels), row_sides)
    wait_halo(own, corners)
    couple(0, [(row, col) for row in range(patch // 2) for col in (0, last)])
    for dr, dc in moves:
        top_copy(dr, dc, (row_index - dr) % across, (col_index - dc) % along).wait_recv()
    for is_late, numbers in enumerate((early, late)):
        for number in numbers:

            @pl.when(inside(-SIDES[number][0], -SIDES[number][1]))
            def _():
                sample_copy(number, is_late).wait_recv()

    def window(ref, row, col):
        return jnp.concatenate(
            [ref[row + code, col + step] for code in range(6) for step in range(3)], axis=-1
        )

    uppers[0][...] = jnp.zeros(uppers[0].shape, BF16)
    for row in range(across):
        for col in range(along // 2):
            even, odd = (tops[row, 2 * col + bit].astype(F32) for bit in range(2))
            low = low_half(even.shape, rank)
            first = jnp.where(low, even, pltpu.roll(odd, rank, 1))
            second = jnp.where(low, pltpu.roll(even, rank, 1), odd)
            both = jnp.concatenate([first, second], axis=0)
            uppers[0][row + 2, col + 1] = both.astype(BF16)
    top_matrix = twice(transfer[levels])
    for step in range(steps - 1):
        child, parent = uppers[step], uppers[step + 1]
        parent[...] = jnp.zeros(parent.shape, BF16)
        rows, cols = across >> step, along >> (step + 1)
        grouped = jnp.concatenate(
            [
                jnp.concatenate(
                    [child[2 * row + 2, 1 : 1 + cols], child[2 * row + 3, 1 : 1 + cols]], axis=-1
                ).reshape(-1, 4 * rank)
                for row in range(rows // 2)
            ],
            axis=0,
        )
        lifted = dot(grouped, top_matrix, NT).reshape(rows // 2, cols * vectors, lanes)
        for row in range(rows // 2):
            parent[row + 2, 1 : 1 + cols // 2] = pair_columns(lifted[row], vectors, rank)
    low = low_half((vectors, lanes), rank)
    upper_images = []
    for step in range(steps):
        row, col = row_index // 2**step, col_index // 2**step
        slab = window(uppers[step], 2 * (row // 2), col // 2)
        mask = jnp.broadcast_to(upper_masks[step : step + 1, :], (16, 36 * rank)).astype(BF16)
        slab = (slab.reshape(-1, 16, 36 * rank) * mask[None]).reshape(slab.shape)
        flat = jnp.concatenate(
            [coupling[col % 2, levels, code + 1 - row % 2, :, 0 : 6 * rank] for code in range(6)],
            axis=-1,
        )
        upper_images.append(dot(slab, twice(flat), NT))
    for level in range(1, levels):
        size = patch >> (level + 1)
        couple(level, [(row, col) for row in range(size) for col in range(size)])
    down = upper_images[-1]
    for step in range(steps - 2, -1, -1):
        row, col = row_index // 2**step, col_index // 2**step
        carried = dot(down.astype(BF16) * low_lanes, top_matrix, NN)
        part = jnp.where(row % 2 == 0, carried[:, :lanes], carried[:, lanes:])
        part = jnp.where(low == (col % 2 == 0), part, pltpu.roll(part, rank, 1))
        down = upper_images[step] + part

    for level in range(levels - 1, -1, -1):
        size = patch >> (level + 1)
        if level == levels - 1:
            parent = down.astype(BF16) * low_lanes
        else:
            parent = jnp.concatenate(
                [split_columns(downs[level + 1][row], rank) for row in range(size)], axis=0
            )
        carried = dot(parent, twice(transfer[level]), NN)
        carried = carried.reshape(size, size, vectors, 2 * lanes)
        for row in range(size):
            for row_bit in range(2):
                spot = 2 * row + row_bit
                part = carried[row, :, :, row_bit * lanes : (row_bit + 1) * lanes]
                downs[level][spot] = (images[level][spot] + part).astype(BF16)

    for side, column, step in ((0, 0, 0), (1, patch - 1, 2)):
        left = jnp.concatenate(
            [col_rims[side, part : part + patch, 0].reshape(-1, sources) for part in range(3)],
            axis=-1,
        )
        flat = jnp.concatenate([near[3 * part + step] for part in range(3)], axis=-1)
        spot = pl.ds(column * vectors, vectors)
        extra = dot(left, flat, NT).reshape(patch, vectors, sources)
        near_sum[:, spot, :] = near_sum[:, spot, :] + extra
    for side, row, step in ((0, 0, 0), (1, patch - 1, 6)):
        left = jnp.concatenate(
            [row_rims[side, part : part + patch].reshape(-1, sources) for part in range(3)],
            axis=-1,
        )
        flat = jnp.concatenate([near[step + part] for part in range(3)], axis=-1)
        near_sum[row] = near_sum[row] + dot(left, flat, NT)

    for is_late, numbers in enumerate((early, late)):
        for number in numbers:

            @pl.when(inside(*SIDES[number]))
            def _():
                sample_copy(number, is_late).wait_send()

    for number in range(len(SIDES)):

        @pl.when(sends(number))
        def _():
            for level in range(levels):
                halo_copy(level, number).wait_send()

    for dr, dc in moves:
        top_copy(dr, dc).wait_send()


def finish_kernel(rank, near_sum, down, basis, out_hbm, out, sems):
    patch, _, vectors, sources = out.shape
    chunks = sems.shape[0]
    rows = patch // chunks
    basis2 = twice(basis[...])

    def rows_out(number):
        spot = pl.ds(number * rows, rows)
        return pltpu.make_async_copy(out.at[spot], out_hbm.at[spot], sems.at[number])

    def body(number, carry):
        spot = pl.ds(number * rows, rows)
        far = split_columns(down[spot].reshape(-1, vectors, 2 * rank), rank)
        summed = near_sum[spot].reshape(-1, sources) + dot(far, basis2, NN)
        out[spot] = summed.astype(BF16).reshape(rows, patch, vectors, sources)
        rows_out(number).start()
        return carry

    lax.fori_loop(0, chunks, body, 0)

    def end(number, carry):
        rows_out(number).wait()
        return carry

    lax.fori_loop(0, chunks, end, 0)


def shards(
    samples,
    leaf_basis,
    transfer,
    coupling,
    near_tiles,
    codes_local,
    counts_local,
    codes_upper,
    counts_upper,
):
    patch, _, vectors, sources = samples.shape
    rank = leaf_basis.shape[0]
    levels = transfer.shape[0] - 1
    lanes = 2 * rank
    across, along = lax.axis_size("gx"), lax.axis_size("gy")
    steps = 1
    while across >> steps >= 2:
        steps += 1
    hbm = pl.BlockSpec(memory_space=pltpu.MemorySpace.HBM)
    vmem = pl.BlockSpec(memory_space=pltpu.VMEM)
    slots = codes_local.shape[-1]
    codes = codes_local.reshape(-1, slots)
    listed_counts = counts_local.transpose(0, 2, 1).reshape(-1, patch)
    far_table, upper_table = spread_tables(rank)

    shapes = [(patch >> level, patch >> (level + 1), vectors, lanes) for level in range(levels)]
    near_sum, down, basis = pl.pallas_call(
        functools.partial(main_kernel, levels, rank, steps, (across, along)),
        out_shape=[
            pltpu.VMEM((patch, patch * vectors, sources), F32),
            pltpu.VMEM(shapes[0], BF16),
            pltpu.VMEM(leaf_basis.shape, BF16),
        ],
        in_specs=[hbm] * 4 + [pl.BlockSpec(memory_space=pltpu.SMEM)] + [hbm] * 6,
        out_specs=[vmem] * 3,
        scratch_shapes=[
            pltpu.VMEM((patch + 2, patch + 2, vectors, sources), BF16),
            pltpu.VMEM(codes.shape, jnp.int32),
            pltpu.VMEM(listed_counts.shape, jnp.int32),
            pltpu.VMEM(codes_upper.shape[::-1], jnp.int32),
            pltpu.VMEM((2, patch + 2, vectors, sources), BF16),
            pltpu.VMEM(transfer.shape, BF16),
            pltpu.VMEM((2, *coupling.shape), BF16),
            pltpu.VMEM(near_tiles.shape, BF16),
            pltpu.VMEM(far_table.shape, BF16),
            pltpu.VMEM(upper_table.shape, BF16),
            pltpu.SemaphoreType.DMA((9 + patch // 4,)),
            pltpu.VMEM((4, GROUP, GROUP), F32),
            pltpu.VMEM((GROUP, GROUP), F32),
            pltpu.VMEM((32, 4 * GROUP), F32),
            pltpu.VMEM((4, KEPT, PAIR_COUNT * lanes), F32),
            pltpu.VMEM((8, 36 * rank), F32),
            pltpu.VMEM((across, along, vectors // 2, lanes), BF16),
            pltpu.VMEM((2, patch + 2, 1, vectors, sources), BF16),
            pltpu.SemaphoreType.DMA((levels + 2, len(SIDES))),
            pltpu.SemaphoreType.DMA((levels + 2, len(SIDES))),
            pltpu.SemaphoreType.DMA((across * along,)),
            pltpu.SemaphoreType.DMA((across * along,)),
        ]
        + [pltpu.VMEM((rows + 4, cols + 2, vectors, lanes), BF16) for rows, cols, _, _ in shapes]
        + [pltpu.VMEM((rows // 2, cols + 2, vectors, lanes), BF16) for rows, cols, _, _ in shapes]
        + [pltpu.VMEM(shape, F32) for shape in shapes]
        + [
            pltpu.VMEM(((across >> step) + 4, (along >> (step + 1)) + 2, vectors, lanes), BF16)
            for step in range(steps)
        ]
        + [pltpu.VMEM(shape, BF16) for shape in shapes[1:]],
        compiler_params=pltpu.CompilerParams(
            collective_id=0, has_side_effects=True, vmem_limit_bytes=VMEM_LIMIT
        ),
        name="main",
    )(
        samples,
        codes,
        listed_counts,
        codes_upper.T,
        counts_upper,
        leaf_basis,
        transfer,
        coupling,
        near_tiles,
        jnp.asarray(far_table),
        jnp.asarray(upper_table),
    )
    return pl.pallas_call(
        functools.partial(finish_kernel, rank),
        out_shape=jax.ShapeDtypeStruct(samples.shape, BF16),
        in_specs=[vmem] * 3,
        out_specs=hbm,
        scratch_shapes=[
            pltpu.VMEM(samples.shape, BF16),
            pltpu.SemaphoreType.DMA((patch // 2,)),
        ],
        compiler_params=pltpu.CompilerParams(vmem_limit_bytes=FINISH_LIMIT),
        name="finish",
    )(near_sum, down, basis)


def solution(mesh):
    placed = (
        P("gx", "gy", None, None),
        P(),
        P(),
        P(),
        P(),
        P("gx", "gy", None, None),
        P("gx", "gy", None),
        P(),
        P(),
    )
    return jax.shard_map(
        shards, mesh=mesh, in_specs=placed, out_specs=P("gx", "gy", None, None), check_vma=False
    )
```

```python
import functools

import jax
import jax.numpy as jnp
import numpy as np
from jax import lax
from jax.experimental import pallas as pl
from jax.experimental.pallas import tpu as pltpu
from jax.sharding import PartitionSpec as P

MESH = pl.DeviceIdType.MESH
F32 = jnp.float32
BF16 = jnp.bfloat16
NT = (((1,), (1,)), ((), ()))
NN = (((1,), (0,)), ((), ()))
VMEM_LIMIT = 50 * 1024 * 1024
AXES = ("gx", "gy")
SIDES = [(sx, sy) for sx in (-1, 0, 1) for sy in (-1, 0, 1) if (sx, sy) != (0, 0)]


def dot(a, b, dims):
    return lax.dot_general(a, b, dims, preferred_element_type=F32)


def twice(matrix):
    return jnp.concatenate([matrix, matrix], axis=0)


def low_half(shape, rank):
    return lax.broadcasted_iota(jnp.int32, shape, len(shape) - 1) < rank


def pair_columns(wide, vectors, rank, swap=False):
    pairs = wide.reshape(-1, 2, vectors, 2 * rank)
    even, odd = (pairs[:, 1], pairs[:, 0]) if swap else (pairs[:, 0], pairs[:, 1])
    return jnp.where(low_half(even.shape, rank), even, odd).astype(BF16)


def split_columns(paired, rank):
    count, vectors, lanes = paired.shape
    low = low_half((1, lanes), rank).astype(F32).astype(BF16)
    both = jnp.stack([paired * low, paired * (1 - low)], axis=1)
    return both.reshape(count * 2 * vectors, lanes)


def span(side, size, width):
    if side == 0:
        return pl.ds(0, size), pl.ds(width, size)
    if side > 0:
        return pl.ds(size - width, width), pl.ds(0, width)
    return pl.ds(0, width), pl.ds(width + size, width)


FINISH_LIMIT = 16 * 1024 * 1024
SHARED = 2


def far_pairs(row_bit, col_bit):
    near_rows = [1 + row_bit, 2 + row_bit, 3 + row_bit]
    far_rows = [row for row in range(6) if row not in near_rows]
    full, single = (2, 0) if col_bit == 0 else (0, 2)
    cells = [(row, pair) for row in far_rows for pair in range(3)]
    cells += [(row, full) for row in near_rows]
    entries = [("full", r, p, None, 6 * r + 2 * p, 6 * r + 2 * p + 1) for r, p in cells]
    first, last = [row for row in near_rows if row != SHARED]
    column = 0 if col_bit == 0 else 5
    codes = [6 * first + column, 6 * SHARED + column]
    low, high = codes if col_bit == 0 else codes[::-1]
    entries.append(("both", first, single, SHARED, low, high))
    code = 6 * last + column
    low, high = (code, -1) if col_bit == 0 else (-1, code)
    entries.append(("half", last, single, None, low, high))
    return entries


PARITIES = [(row_bit, col_bit) for row_bit in range(2) for col_bit in range(2)]
PAIRS = {parity: far_pairs(*parity) for parity in PARITIES}
PAIR_COUNT = len(PAIRS[0, 0])
CODE_ROWS = 48
GROUP = 128
KEPT = 96


def spread_tables(rank):
    def table(codes):
        lanes = np.repeat(np.array(codes), rank)
        return (np.arange(CODE_ROWS)[:, None] == lanes[None]).astype(np.float32)

    far = [table([c for e in PAIRS[p] for c in e[4:6]]) for p in PARITIES]
    return np.stack(far).astype(BF16), table(range(36)).astype(BF16)


def main_kernel(levels, rank, steps, counts, *refs):
    (samples_hbm, codes_hbm, counts_hbm, codes_upper_hbm, counts_upper) = refs[:5]
    (basis_hbm, transfer_hbm, coupling_hbm, near_hbm, table_hbm, table_upper_hbm) = refs[5:11]
    near_sum, leaf_down, basis = refs[11:14]
    scratch = refs[14:]
    (samples, codes, listed_counts, codes_upper) = scratch[:4]
    (row_rims, transfer, coupling, near, table, table_upper) = scratch[4:10]
    local, codes_flat, turned_counts, turned, masks, upper_masks = scratch[10:16]
    tops, col_rims, send, recv, top_send, top_recv = scratch[16:22]
    scratch = scratch[22:]
    padded, swapped, images = scratch[:levels], scratch[levels : 2 * levels], scratch[2 * levels : 3 * levels]
    uppers = scratch[3 * levels : 3 * levels + steps]
    downs = (leaf_down, *scratch[3 * levels + steps :])
    patch, _, vectors, sources = samples_hbm.shape
    across, along = counts
    lanes = 2 * rank
    row_index, col_index = lax.axis_index("gx"), lax.axis_index("gy")

    chunk = 8
    fetch = [
        (codes_hbm, codes),
        (counts_hbm, listed_counts),
        (codes_upper_hbm, codes_upper),
        (coupling_hbm, coupling.at[1]),
        (basis_hbm, basis),
        (table_hbm, table),
        (table_upper_hbm, table_upper),
        (transfer_hbm, transfer),
        (near_hbm, near),
    ]
    names = ["codes", "counts", "upper", "coupling", "basis"]
    names += ["table", "table_upper", "transfer", "near"]
    fetch = {
        name: pltpu.make_async_copy(*pair, local.at[number])
        for number, (name, pair) in enumerate(zip(names, fetch))
    }

    def rows_in(number):
        return pltpu.make_async_copy(
            samples_hbm.at[pl.ds(number * chunk, chunk)],
            samples.at[pl.ds(1 + number * chunk, chunk), pl.ds(1, patch)],
            local.at[len(names) + number],
        )

    for name in ("codes", "counts", "upper", "table", "table_upper", "basis"):
        fetch[name].start()
    for number in range(patch // chunk):
        rows_in(number).start()
    for name in ("transfer", "coupling", "near"):
        fetch[name].start()

    def clear_border(target, height, width):
        rows, cols, *tail = target.shape
        for top, tall, left, wide in (
            (0, height, 0, cols),
            (rows - height, height, 0, cols),
            (height, rows - 2 * height, 0, width),
            (height, rows - 2 * height, cols - width, width),
        ):
            target[top : top + tall, left : left + wide] = jnp.zeros((tall, wide, *tail), BF16)

    clear_border(samples, 1, 1)
    row_rims[...] = jnp.zeros(row_rims.shape, BF16)
    col_rims[...] = jnp.zeros(col_rims.shape, BF16)
    for level in range(levels):
        clear_border(padded[level], 2, 1)

    there_rows = [(row_index + step) % across for step in range(across)]
    there_cols = [(col_index + step) % along for step in range(along)]
    moves = [(dr, dc) for dr in range(across) for dc in range(along) if (dr, dc) != (0, 0)]
    barrier = pltpu.get_barrier_semaphore()
    for dr, dc in moves:
        pl.semaphore_signal(
            barrier, inc=1, device_id=(there_rows[dr], there_cols[dc]), device_id_type=MESH
        )

    def top_copy(dr, dc, from_row=None, from_col=None):
        from_row = row_index if from_row is None else from_row
        from_col = col_index if from_col is None else from_col
        return pltpu.make_async_remote_copy(
            src_ref=tops.at[row_index, col_index],
            dst_ref=tops.at[from_row, from_col],
            send_sem=top_send.at[dr * along + dc],
            recv_sem=top_recv.at[dr * along + dc],
            device_id=(there_rows[dr], there_cols[dc]),
            device_id_type=MESH,
        )

    def halo_copy(level, number):
        sx, sy = SIDES[number]
        ref = padded[level]
        rows_from, rows_to = span(sx, patch >> level, 2)
        cols_from, cols_to = span(sy, patch >> (level + 1), 1)
        rows_from = pl.ds(rows_from.start + 2, rows_from.size)
        corner = sx != 0 and sy != 0
        cols_from = cols_to if corner else pl.ds(cols_from.start + 1, cols_from.size)
        return pltpu.make_async_remote_copy(
            src_ref=ref.at[rows_from, cols_from],
            dst_ref=ref.at[rows_to, cols_to],
            send_sem=send.at[level, number],
            recv_sem=recv.at[level, number],
            device_id=(row_index + sx, col_index if corner else col_index + sy),
            device_id_type=MESH,
        )

    def rim_spot(number, late):
        sx, sy = SIDES[number]
        _, cols_to = span(sy, patch, 1)
        if sx == 0:
            return col_rims.at[0 if sy > 0 else 1, pl.ds(1 + late * (patch // 2), patch // 2)]
        return row_rims.at[pl.ds(0 if sx > 0 else 1, 1), cols_to]

    def sample_copy(number, late):
        sx, sy = SIDES[number]
        rows_from, _ = span(sx, patch, 1)
        cols_from, _ = span(sy, patch, 1)
        if sx == 0:
            rows_from = pl.ds(late * (patch // 2), patch // 2)
        return pltpu.make_async_remote_copy(
            src_ref=samples_hbm.at[rows_from, cols_from],
            dst_ref=rim_spot(number, late),
            send_sem=send.at[levels + late, number],
            recv_sem=recv.at[levels + late, number],
            device_id=(row_index + sx, col_index + sy),
            device_id_type=MESH,
        )

    def inside(sx, sy):
        there_row, there_col = row_index + sx, col_index + sy
        return (there_row >= 0) & (there_row < across) & (there_col >= 0) & (there_col < along)

    numbered = list(enumerate(SIDES))
    column_sides = [n for n, (sx, sy) in numbered if sx == 0]
    row_sides = [n for n, (sx, sy) in numbered if sy == 0]
    corners = [n for n, (sx, sy) in numbered if sx != 0 and sy != 0]

    def sends(number):
        sx, sy = SIDES[number]
        return inside(sx, 0) & inside(0, -sy) if number in corners else inside(sx, sy)

    early = column_sides
    late = column_sides + row_sides + corners

    def start_samples(numbers, is_late):
        for number in numbers:

            @pl.when(inside(*SIDES[number]))
            def _():
                sample_copy(number, is_late).start()

    def start_halo(which, numbers):
        for number in numbers:

            @pl.when(sends(number))
            def _():
                for level in which:
                    halo_copy(level, number).start()

    def wait_halo(which, numbers):
        for number in numbers:
            sx, sy = SIDES[number]

            @pl.when(inside(-sx, -sy))
            def _():
                for level in which:
                    halo_copy(level, number).wait_recv()

    fetch["codes"].wait()
    fetch["counts"].wait()
    slots = codes.shape[-1]
    turned_counts[0 : listed_counts.shape[0], 0:patch] = listed_counts[...].astype(F32)
    turned_counts[...] = jnp.transpose(turned_counts[...])
    codes_flat[...] = jnp.full(codes_flat.shape, -1.0, F32)
    slot_lane = lax.broadcasted_iota(jnp.int32, (patch // 2, slots), 1).astype(F32)
    starts = [0]
    for level in range(levels):
        starts.append(starts[-1] + (patch >> (level + 1)) ** 2)
    for level in range(levels):
        size = patch >> level
        half = size // 2
        for row in range(size):
            for bit in range(2):
                begin = ((row << level) * patch + (bit << level)) * levels + level
                if half > 1:
                    listed = codes[pl.ds(begin, half, stride=levels << (level + 1)), :]
                    column = pl.ds(bit << level, half, stride=2 << level)
                else:
                    listed = codes[pl.ds(begin, 1), :]
                    column = pl.ds(bit << level, 1)
                lane = (row << level) * levels + level
                count = turned_counts[column, :][:, lane : lane + 1]
                spot = starts[level] + (row // 2) * half
                codes_flat[row % 2 * 2 + bit, spot : spot + half, 0:slots] = jnp.where(
                    slot_lane[:half] < count, listed.astype(F32), -1.0
                )
    fetch["upper"].wait()
    turns = [jnp.transpose(codes_flat[parity])[0:slots] for parity in range(4)]
    begin = 0
    upper_codes = codes_upper[...].astype(F32)
    upper_lane = lax.broadcasted_iota(jnp.int32, upper_codes.shape, 1)
    slot_row = lax.broadcasted_iota(jnp.int32, (slots, 1), 0)
    group_lane = lax.broadcasted_iota(jnp.int32, (slots, GROUP), 1)
    for step in range(steps):
        cols = along >> step
        index = begin + (row_index // 2**step) * cols + col_index // 2**step
        listed = jnp.sum(jnp.where(upper_lane == index, upper_codes, 0.0), axis=1, keepdims=True)
        listed = jnp.where(slot_row < counts_upper[index], listed, -1.0)
        turns[0] = jnp.where(group_lane == KEPT - 8 + step, listed, turns[0])
        begin += (across >> step) * cols
    for parity in range(4):
        turned[0:slots, parity * GROUP : (parity + 1) * GROUP] = turns[parity]
    code = lax.broadcasted_iota(jnp.int32, (CODE_ROWS, GROUP), 0).astype(F32)
    founds = []
    for parity in range(4):
        found = jnp.zeros((GROUP, GROUP), F32)[0:CODE_ROWS]
        for slot in range(slots):
            listed = turned[slot : slot + 1, parity * GROUP : (parity + 1) * GROUP]
            found = jnp.where(code == listed, 1.0, found)
        found = jnp.concatenate([found, jnp.zeros((GROUP - CODE_ROWS, GROUP), F32)], axis=0)
        founds.append(jnp.transpose(found)[0:KEPT, 0:CODE_ROWS].astype(BF16))
    fetch["table"].wait()
    fetch["table_upper"].wait()
    for parity in range(4):
        masks[parity] = dot(founds[parity], table[parity], NN)
    upper_masks[...] = dot(founds[0][KEPT - 16 :], table_upper[...], NN)[8:]

    pl.semaphore_wait(barrier, len(moves))

    fetch["basis"].wait()
    own_basis = twice(basis[...])

    def project(number, carry):
        rows_in(number).wait()
        rows = samples[pl.ds(1 + number * chunk, chunk), 1 : 1 + patch].reshape(-1, sources)
        wide = dot(rows, own_basis, NT).reshape(chunk, patch * vectors, lanes)
        for row in range(chunk):
            padded[0][number * chunk + row + 2, 1 : 1 + patch // 2] = pair_columns(
                wide[row], vectors, rank
            )
            if row % 2 == 0:
                swapped[0][number * (chunk // 2) + row // 2, 1 : 1 + patch // 2] = pair_columns(
                    wide[row], vectors, rank, True
                )
        return carry

    lax.fori_loop(0, patch // chunk, project, 0)
    start_halo([0], column_sides + row_sides)
    fetch["transfer"].wait()

    for level in range(levels):
        child = padded[level]
        matrix = twice(transfer[level])
        cols = patch >> (level + 1)
        grouped = jnp.concatenate(
            [
                jnp.concatenate(
                    [child[2 * row + 2, 1 : 1 + cols], child[2 * row + 3, 1 : 1 + cols]], axis=-1
                ).reshape(-1, 4 * rank)
                for row in range(cols)
            ],
            axis=0,
        )
        lifted = dot(grouped, matrix, NT)
        if level < levels - 1:
            lifted = lifted.reshape(cols, cols * vectors, lanes)
            for row in range(cols):
                padded[level + 1][row + 2, 1 : 1 + cols // 2] = pair_columns(
                    lifted[row], vectors, rank
                )
                if row % 2 == 0:
                    swapped[level + 1][row // 2, 1 : 1 + cols // 2] = pair_columns(
                        lifted[row], vectors, rank, True
                    )
        else:
            half = vectors // 2
            tops[row_index, col_index] = jnp.where(
                low_half((half, lanes), rank), lifted[:half], lifted[half:]
            ).astype(BF16)

    start_halo(range(levels - 1, 0, -1), column_sides + row_sides)
    for dr, dc in moves:
        top_copy(dr, dc).start()

    fetch["coupling"].wait()

    def shift(level, carry):
        for part in range(coupling.shape[2]):
            coupling[0, level, part, :, 0 : 6 * rank] = coupling[1, level, part, :, rank : 7 * rank]
        return carry

    lax.fori_loop(0, coupling.shape[1], shift, 0)
    low_lanes = low_half((1, lanes), rank).astype(F32).astype(BF16)
    high_lanes = 1 - low_lanes

    def weights(level, row_bit):
        sides = []
        for col_bit in range(2):
            parts = []
            for kind, row, pair, other, _, _ in PAIRS[row_bit, col_bit]:
                spot = pl.ds(pair * lanes, lanes)
                part = coupling[col_bit, level, row + 1 - row_bit, :, spot]
                if kind == "both":
                    second = coupling[1 - col_bit, level, other + 1 - row_bit, :, spot]
                    if col_bit == 0:
                        part = part * low_lanes + second * high_lanes
                    else:
                        part = part * high_lanes + second * low_lanes
                parts.append(part)
            parts = jnp.concatenate(parts, axis=-1)
            blank = jnp.zeros_like(parts)
            sides.append(jnp.concatenate([parts, blank] if col_bit == 0 else [blank, parts], axis=0))
        return jnp.concatenate(sides, axis=-1)

    def couple(level, cells):
        cols = patch >> (level + 1)
        for row_bit in range(2):
            left = []
            for row, col in cells:
                line = []
                for col_bit in range(2):
                    spot = starts[level] + row * cols + col
                    mask = masks[row_bit * 2 + col_bit, pl.ds(spot, 1), :]
                    mask = jnp.broadcast_to(mask, (16, PAIR_COUNT * lanes)).astype(BF16)
                    parts = []
                    for kind, part_row, pair, _, _, _ in PAIRS[row_bit, col_bit]:
                        part = padded[level][2 * row + part_row, col + pair]
                        if kind == "both":
                            second = swapped[level][row, col + pair]
                            if col_bit == 0:
                                part = part * low_lanes + second * high_lanes
                            else:
                                part = part * high_lanes + second * low_lanes
                        parts.append(part)
                    parts = jnp.concatenate(parts, axis=-1)
                    parts = parts.reshape(-1, 16, PAIR_COUNT * lanes) * mask[None]
                    line.append(parts.reshape(vectors, PAIR_COUNT * lanes))
                left.append(jnp.concatenate(line, axis=-1))
            image = dot(jnp.concatenate(left, axis=0), weights(level, row_bit), NT)
            image = image.reshape(len(cells), vectors, lanes)
            for number, (row, col) in enumerate(cells):
                images[level][2 * row + row_bit, col] = image[number]

    inner = range(1, patch // 2 - 1)

    def inner_rows(pair, carry):
        couple(0, [(1 + 2 * pair + step, col) for step in range(2) for col in inner])
        return carry

    lax.fori_loop(0, len(inner) // 2, inner_rows, 0)

    last = patch // 2 - 1
    own = range(levels)
    wait_halo([0], row_sides)
    couple(0, [(row, col) for row in (0, last) for col in inner])
    fetch["near"].wait()
    strip = 2

    def near_body(number, carry):
        spot = pl.ds(number * strip, strip)
        left = jnp.concatenate(
            [
                samples[pl.ds(number * strip + row, strip), col : col + patch].reshape(-1, sources)
                for row in range(3)
                for col in range(3)
            ],
            axis=-1,
        )
        flat = jnp.concatenate([near[tile] for tile in range(9)], axis=-1)
        near_sum[spot] = dot(left, flat, NT).reshape(strip, patch * vectors, sources)
        return carry

    lax.fori_loop(0, 2, near_body, 0)
    start_samples(early, 0)
    start_samples(late, 1)
    lax.fori_loop(2, patch // strip - 2, near_body, 0)
    wait_halo(own, column_sides)
    start_halo(own, corners)
    lax.fori_loop(patch // strip - 2, patch // strip, near_body, 0)
    for level in range(levels):
        rows, cols = patch >> (level + 1), (patch >> (level + 1)) + 2
        for edge in (0, cols - 1):
            for row in range(rows):
                piece = padded[level][2 * row + 2, edge].astype(F32)
                swapped[level][row, edge] = pltpu.roll(piece, rank, 1).astype(BF16)

    wait_halo(range(1, levels), row_sides)
    wait_halo(own, corners)
    couple(0, [(row, col) for row in range(patch // 2) for col in (0, last)])
    for dr, dc in moves:
        top_copy(dr, dc, (row_index - dr) % across, (col_index - dc) % along).wait_recv()
    for is_late, numbers in enumerate((early, late)):
        for number in numbers:

            @pl.when(inside(-SIDES[number][0], -SIDES[number][1]))
            def _():
                sample_copy(number, is_late).wait_recv()

    def window(ref, row, col):
        return jnp.concatenate(
            [ref[row + code, col + step] for code in range(6) for step in range(3)], axis=-1
        )

    uppers[0][...] = jnp.zeros(uppers[0].shape, BF16)
    for row in range(across):
        for col in range(along // 2):
            even, odd = (tops[row, 2 * col + bit].astype(F32) for bit in range(2))
            low = low_half(even.shape, rank)
            first = jnp.where(low, even, pltpu.roll(odd, rank, 1))
            second = jnp.where(low, pltpu.roll(even, rank, 1), odd)
            both = jnp.concatenate([first, second], axis=0)
            uppers[0][row + 2, col + 1] = both.astype(BF16)
    top_matrix = twice(transfer[levels])
    for step in range(steps - 1):
        child, parent = uppers[step], uppers[step + 1]
        parent[...] = jnp.zeros(parent.shape, BF16)
        rows, cols = across >> step, along >> (step + 1)
        grouped = jnp.concatenate(
            [
                jnp.concatenate(
                    [child[2 * row + 2, 1 : 1 + cols], child[2 * row + 3, 1 : 1 + cols]], axis=-1
                ).reshape(-1, 4 * rank)
                for row in range(rows // 2)
            ],
            axis=0,
        )
        lifted = dot(grouped, top_matrix, NT).reshape(rows // 2, cols * vectors, lanes)
        for row in range(rows // 2):
            parent[row + 2, 1 : 1 + cols // 2] = pair_columns(lifted[row], vectors, rank)
    low = low_half((vectors, lanes), rank)
    upper_images = []
    for step in range(steps):
        row, col = row_index // 2**step, col_index // 2**step
        slab = window(uppers[step], 2 * (row // 2), col // 2)
        mask = jnp.broadcast_to(upper_masks[step : step + 1, :], (16, 36 * rank)).astype(BF16)
        slab = (slab.reshape(-1, 16, 36 * rank) * mask[None]).reshape(slab.shape)
        flat = jnp.concatenate(
            [coupling[col % 2, levels, code + 1 - row % 2, :, 0 : 6 * rank] for code in range(6)],
            axis=-1,
        )
        upper_images.append(dot(slab, twice(flat), NT))
    for level in range(1, levels):
        size = patch >> (level + 1)
        couple(level, [(row, col) for row in range(size) for col in range(size)])
    down = upper_images[-1]
    for step in range(steps - 2, -1, -1):
        row, col = row_index // 2**step, col_index // 2**step
        carried = dot(down.astype(BF16) * low_lanes, top_matrix, NN)
        part = jnp.where(row % 2 == 0, carried[:, :lanes], carried[:, lanes:])
        part = jnp.where(low == (col % 2 == 0), part, pltpu.roll(part, rank, 1))
        down = upper_images[step] + part

    for level in range(levels - 1, -1, -1):
        size = patch >> (level + 1)
        if level == levels - 1:
            parent = down.astype(BF16) * low_lanes
        else:
            parent = jnp.concatenate(
                [split_columns(downs[level + 1][row], rank) for row in range(size)], axis=0
            )
        carried = dot(parent, twice(transfer[level]), NN)
        carried = carried.reshape(size, size, vectors, 2 * lanes)
        for row in range(size):
            for row_bit in range(2):
                spot = 2 * row + row_bit
                part = carried[row, :, :, row_bit * lanes : (row_bit + 1) * lanes]
                downs[level][spot] = (images[level][spot] + part).astype(BF16)

    for side, column, step in ((0, 0, 0), (1, patch - 1, 2)):
        left = jnp.concatenate(
            [col_rims[side, part : part + patch, 0].reshape(-1, sources) for part in range(3)],
            axis=-1,
        )
        flat = jnp.concatenate([near[3 * part + step] for part in range(3)], axis=-1)
        spot = pl.ds(column * vectors, vectors)
        extra = dot(left, flat, NT).reshape(patch, vectors, sources)
        near_sum[:, spot, :] = near_sum[:, spot, :] + extra
    for side, row, step in ((0, 0, 0), (1, patch - 1, 6)):
        left = jnp.concatenate(
            [row_rims[side, part : part + patch].reshape(-1, sources) for part in range(3)],
            axis=-1,
        )
        flat = jnp.concatenate([near[step + part] for part in range(3)], axis=-1)
        near_sum[row] = near_sum[row] + dot(left, flat, NT)

    for is_late, numbers in enumerate((early, late)):
        for number in numbers:

            @pl.when(inside(*SIDES[number]))
            def _():
                sample_copy(number, is_late).wait_send()

    for number in range(len(SIDES)):

        @pl.when(sends(number))
        def _():
            for level in range(levels):
                halo_copy(level, number).wait_send()

    for dr, dc in moves:
        top_copy(dr, dc).wait_send()


def finish_kernel(rank, near_sum, down, basis, out_hbm, out, sems):
    patch, _, vectors, sources = out.shape
    chunks = sems.shape[0]
    rows = patch // chunks
    basis2 = twice(basis[...])

    def rows_out(number):
        spot = pl.ds(number * rows, rows)
        return pltpu.make_async_copy(out.at[spot], out_hbm.at[spot], sems.at[number])

    def body(number, carry):
        spot = pl.ds(number * rows, rows)
        far = split_columns(down[spot].reshape(-1, vectors, 2 * rank), rank)
        summed = near_sum[spot].reshape(-1, sources) + dot(far, basis2, NN)
        out[spot] = summed.astype(BF16).reshape(rows, patch, vectors, sources)
        rows_out(number).start()
        return carry

    lax.fori_loop(0, chunks, body, 0)

    def end(number, carry):
        rows_out(number).wait()
        return carry

    lax.fori_loop(0, chunks, end, 0)


def shards(
    samples,
    leaf_basis,
    transfer,
    coupling,
    near_tiles,
    codes_local,
    counts_local,
    codes_upper,
    counts_upper,
):
    patch, _, vectors, sources = samples.shape
    rank = leaf_basis.shape[0]
    levels = transfer.shape[0] - 1
    lanes = 2 * rank
    across, along = lax.axis_size("gx"), lax.axis_size("gy")
    steps = 1
    while across >> steps >= 2:
        steps += 1
    hbm = pl.BlockSpec(memory_space=pltpu.MemorySpace.HBM)
    vmem = pl.BlockSpec(memory_space=pltpu.VMEM)
    slots = codes_local.shape[-1]
    codes = codes_local.reshape(-1, slots)
    listed_counts = counts_local.transpose(0, 2, 1).reshape(-1, patch)
    far_table, upper_table = spread_tables(rank)

    shapes = [(patch >> level, patch >> (level + 1), vectors, lanes) for level in range(levels)]
    near_sum, down, basis = pl.pallas_call(
        functools.partial(main_kernel, levels, rank, steps, (across, along)),
        out_shape=[
            pltpu.VMEM((patch, patch * vectors, sources), F32),
            pltpu.VMEM(shapes[0], BF16),
            pltpu.VMEM(leaf_basis.shape, BF16),
        ],
        in_specs=[hbm] * 4 + [pl.BlockSpec(memory_space=pltpu.SMEM)] + [hbm] * 6,
        out_specs=[vmem] * 3,
        scratch_shapes=[
            pltpu.VMEM((patch + 2, patch + 2, vectors, sources), BF16),
            pltpu.VMEM(codes.shape, jnp.int32),
            pltpu.VMEM(listed_counts.shape, jnp.int32),
            pltpu.VMEM(codes_upper.shape[::-1], jnp.int32),
            pltpu.VMEM((2, patch + 2, vectors, sources), BF16),
            pltpu.VMEM(transfer.shape, BF16),
            pltpu.VMEM((2, *coupling.shape), BF16),
            pltpu.VMEM(near_tiles.shape, BF16),
            pltpu.VMEM(far_table.shape, BF16),
            pltpu.VMEM(upper_table.shape, BF16),
            pltpu.SemaphoreType.DMA((9 + patch // 4,)),
            pltpu.VMEM((4, GROUP, GROUP), F32),
            pltpu.VMEM((GROUP, GROUP), F32),
            pltpu.VMEM((32, 4 * GROUP), F32),
            pltpu.VMEM((4, KEPT, PAIR_COUNT * lanes), F32),
            pltpu.VMEM((8, 36 * rank), F32),
            pltpu.VMEM((across, along, vectors // 2, lanes), BF16),
            pltpu.VMEM((2, patch + 2, 1, vectors, sources), BF16),
            pltpu.SemaphoreType.DMA((levels + 2, len(SIDES))),
            pltpu.SemaphoreType.DMA((levels + 2, len(SIDES))),
            pltpu.SemaphoreType.DMA((across * along,)),
            pltpu.SemaphoreType.DMA((across * along,)),
        ]
        + [pltpu.VMEM((rows + 4, cols + 2, vectors, lanes), BF16) for rows, cols, _, _ in shapes]
        + [pltpu.VMEM((rows // 2, cols + 2, vectors, lanes), BF16) for rows, cols, _, _ in shapes]
        + [pltpu.VMEM(shape, F32) for shape in shapes]
        + [
            pltpu.VMEM(((across >> step) + 4, (along >> (step + 1)) + 2, vectors, lanes), BF16)
            for step in range(steps)
        ]
        + [pltpu.VMEM(shape, BF16) for shape in shapes[1:]],
        compiler_params=pltpu.CompilerParams(
            collective_id=0, has_side_effects=True, vmem_limit_bytes=VMEM_LIMIT
        ),
        name="main",
    )(
        samples,
        codes,
        listed_counts,
        codes_upper.T,
        counts_upper,
        leaf_basis,
        transfer,
        coupling,
        near_tiles,
        jnp.asarray(far_table),
        jnp.asarray(upper_table),
    )
    return pl.pallas_call(
        functools.partial(finish_kernel, rank),
        out_shape=jax.ShapeDtypeStruct(samples.shape, BF16),
        in_specs=[vmem] * 3,
        out_specs=hbm,
        scratch_shapes=[
            pltpu.VMEM(samples.shape, BF16),
            pltpu.SemaphoreType.DMA((patch // 4,)),
        ],
        compiler_params=pltpu.CompilerParams(vmem_limit_bytes=FINISH_LIMIT),
        name="finish",
    )(near_sum, down, basis)


def solution(mesh):
    placed = (
        P("gx", "gy", None, None),
        P(),
        P(),
        P(),
        P(),
        P("gx", "gy", None, None),
        P("gx", "gy", None),
        P(),
        P(),
    )
    return jax.shard_map(
        shards, mesh=mesh, in_specs=placed, out_specs=P("gx", "gy", None, None), check_vma=False
    )
```

```python
import functools

import jax
import jax.numpy as jnp
import numpy as np
from jax import lax
from jax.experimental import pallas as pl
from jax.experimental.pallas import tpu as pltpu
from jax.sharding import PartitionSpec as P

MESH = pl.DeviceIdType.MESH
F32 = jnp.float32
BF16 = jnp.bfloat16
NT = (((1,), (1,)), ((), ()))
NN = (((1,), (0,)), ((), ()))
VMEM_LIMIT = 50 * 1024 * 1024
AXES = ("gx", "gy")
SIDES = [(sx, sy) for sx in (-1, 0, 1) for sy in (-1, 0, 1) if (sx, sy) != (0, 0)]


def dot(a, b, dims):
    return lax.dot_general(a, b, dims, preferred_element_type=F32)


def twice(matrix):
    return jnp.concatenate([matrix, matrix], axis=0)


def low_half(shape, rank):
    return lax.broadcasted_iota(jnp.int32, shape, len(shape) - 1) < rank


def pair_columns(wide, vectors, rank, swap=False):
    pairs = wide.reshape(-1, 2, vectors, 2 * rank)
    even, odd = (pairs[:, 1], pairs[:, 0]) if swap else (pairs[:, 0], pairs[:, 1])
    return jnp.where(low_half(even.shape, rank), even, odd).astype(BF16)


def split_columns(paired, rank):
    count, vectors, lanes = paired.shape
    low = low_half((1, lanes), rank).astype(F32).astype(BF16)
    both = jnp.stack([paired * low, paired * (1 - low)], axis=1)
    return both.reshape(count * 2 * vectors, lanes)


def span(side, size, width):
    if side == 0:
        return pl.ds(0, size), pl.ds(width, size)
    if side > 0:
        return pl.ds(size - width, width), pl.ds(0, width)
    return pl.ds(0, width), pl.ds(width + size, width)


FINISH_LIMIT = 16 * 1024 * 1024
SHARED = 2


def far_pairs(row_bit, col_bit):
    near_rows = [1 + row_bit, 2 + row_bit, 3 + row_bit]
    far_rows = [row for row in range(6) if row not in near_rows]
    full, single = (2, 0) if col_bit == 0 else (0, 2)
    cells = [(row, pair) for row in far_rows for pair in range(3)]
    cells += [(row, full) for row in near_rows]
    entries = [("full", r, p, None, 6 * r + 2 * p, 6 * r + 2 * p + 1) for r, p in cells]
    first, last = [row for row in near_rows if row != SHARED]
    column = 0 if col_bit == 0 else 5
    codes = [6 * first + column, 6 * SHARED + column]
    low, high = codes if col_bit == 0 else codes[::-1]
    entries.append(("both", first, single, SHARED, low, high))
    code = 6 * last + column
    low, high = (code, -1) if col_bit == 0 else (-1, code)
    entries.append(("half", last, single, None, low, high))
    return entries


PARITIES = [(row_bit, col_bit) for row_bit in range(2) for col_bit in range(2)]
PAIRS = {parity: far_pairs(*parity) for parity in PARITIES}
PAIR_COUNT = len(PAIRS[0, 0])
CODE_ROWS = 48
GROUP = 128
KEPT = 96


def spread_tables(rank):
    def table(codes):
        lanes = np.repeat(np.array(codes), rank)
        return (np.arange(CODE_ROWS)[:, None] == lanes[None]).astype(np.float32)

    far = [table([c for e in PAIRS[p] for c in e[4:6]]) for p in PARITIES]
    return np.stack(far).astype(BF16), table(range(36)).astype(BF16)


def main_kernel(levels, rank, steps, counts, *refs):
    (samples_hbm, codes_hbm, counts_hbm, codes_upper_hbm, counts_upper) = refs[:5]
    (basis_hbm, transfer_hbm, coupling_hbm, near_hbm, table_hbm, table_upper_hbm) = refs[5:11]
    near_sum, leaf_down, basis = refs[11:14]
    scratch = refs[14:]
    (samples, codes, listed_counts, codes_upper) = scratch[:4]
    (row_rims, transfer, coupling, near, table, table_upper) = scratch[4:10]
    local, codes_flat, turned_counts, turned, masks, upper_masks = scratch[10:16]
    tops, col_rims, send, recv, top_send, top_recv = scratch[16:22]
    scratch = scratch[22:]
    padded, swapped, images = scratch[:levels], scratch[levels : 2 * levels], scratch[2 * levels : 3 * levels]
    uppers = scratch[3 * levels : 3 * levels + steps]
    downs = (leaf_down, *scratch[3 * levels + steps :])
    patch, _, vectors, sources = samples_hbm.shape
    across, along = counts
    lanes = 2 * rank
    row_index, col_index = lax.axis_index("gx"), lax.axis_index("gy")

    chunk = 8
    fetch = [
        (codes_hbm, codes),
        (counts_hbm, listed_counts),
        (codes_upper_hbm, codes_upper),
        (coupling_hbm, coupling.at[1]),
        (basis_hbm, basis),
        (table_hbm, table),
        (table_upper_hbm, table_upper),
        (transfer_hbm, transfer),
        (near_hbm, near),
    ]
    names = ["codes", "counts", "upper", "coupling", "basis"]
    names += ["table", "table_upper", "transfer", "near"]
    fetch = {
        name: pltpu.make_async_copy(*pair, local.at[number])
        for number, (name, pair) in enumerate(zip(names, fetch))
    }

    def rows_in(number):
        return pltpu.make_async_copy(
            samples_hbm.at[pl.ds(number * chunk, chunk)],
            samples.at[pl.ds(1 + number * chunk, chunk), pl.ds(1, patch)],
            local.at[len(names) + number],
        )

    for name in ("codes", "counts", "upper", "table", "table_upper", "basis"):
        fetch[name].start()
    for number in range(patch // chunk):
        rows_in(number).start()
    for name in ("transfer", "coupling", "near"):
        fetch[name].start()

    def clear_border(target, height, width):
        rows, cols, *tail = target.shape
        for top, tall, left, wide in (
            (0, height, 0, cols),
            (rows - height, height, 0, cols),
            (height, rows - 2 * height, 0, width),
            (height, rows - 2 * height, cols - width, width),
        ):
            target[top : top + tall, left : left + wide] = jnp.zeros((tall, wide, *tail), BF16)

    clear_border(samples, 1, 1)
    row_rims[...] = jnp.zeros(row_rims.shape, BF16)
    col_rims[...] = jnp.zeros(col_rims.shape, BF16)
    for level in range(levels):
        clear_border(padded[level], 2, 1)

    there_rows = [(row_index + step) % across for step in range(across)]
    there_cols = [(col_index + step) % along for step in range(along)]
    moves = [(dr, dc) for dr in range(across) for dc in range(along) if (dr, dc) != (0, 0)]
    barrier = pltpu.get_barrier_semaphore()
    for dr, dc in moves:
        pl.semaphore_signal(
            barrier, inc=1, device_id=(there_rows[dr], there_cols[dc]), device_id_type=MESH
        )

    def top_copy(dr, dc, from_row=None, from_col=None):
        from_row = row_index if from_row is None else from_row
        from_col = col_index if from_col is None else from_col
        return pltpu.make_async_remote_copy(
            src_ref=tops.at[row_index, col_index],
            dst_ref=tops.at[from_row, from_col],
            send_sem=top_send.at[dr * along + dc],
            recv_sem=top_recv.at[dr * along + dc],
            device_id=(there_rows[dr], there_cols[dc]),
            device_id_type=MESH,
        )

    def halo_copy(level, number):
        sx, sy = SIDES[number]
        ref = padded[level]
        rows_from, rows_to = span(sx, patch >> level, 2)
        cols_from, cols_to = span(sy, patch >> (level + 1), 1)
        rows_from = pl.ds(rows_from.start + 2, rows_from.size)
        corner = sx != 0 and sy != 0
        cols_from = cols_to if corner else pl.ds(cols_from.start + 1, cols_from.size)
        return pltpu.make_async_remote_copy(
            src_ref=ref.at[rows_from, cols_from],
            dst_ref=ref.at[rows_to, cols_to],
            send_sem=send.at[level, number],
            recv_sem=recv.at[level, number],
            device_id=(row_index + sx, col_index if corner else col_index + sy),
            device_id_type=MESH,
        )

    def rim_spot(number, late):
        sx, sy = SIDES[number]
        _, cols_to = span(sy, patch, 1)
        if sx == 0:
            return col_rims.at[0 if sy > 0 else 1, pl.ds(1 + late * (patch // 2), patch // 2)]
        return row_rims.at[pl.ds(0 if sx > 0 else 1, 1), cols_to]

    def sample_copy(number, late):
        sx, sy = SIDES[number]
        rows_from, _ = span(sx, patch, 1)
        cols_from, _ = span(sy, patch, 1)
        if sx == 0:
            rows_from = pl.ds(late * (patch // 2), patch // 2)
        return pltpu.make_async_remote_copy(
            src_ref=samples_hbm.at[rows_from, cols_from],
            dst_ref=rim_spot(number, late),
            send_sem=send.at[levels + late, number],
            recv_sem=recv.at[levels + late, number],
            device_id=(row_index + sx, col_index + sy),
            device_id_type=MESH,
        )

    def inside(sx, sy):
        there_row, there_col = row_index + sx, col_index + sy
        return (there_row >= 0) & (there_row < across) & (there_col >= 0) & (there_col < along)

    numbered = list(enumerate(SIDES))
    column_sides = [n for n, (sx, sy) in numbered if sx == 0]
    row_sides = [n for n, (sx, sy) in numbered if sy == 0]
    corners = [n for n, (sx, sy) in numbered if sx != 0 and sy != 0]

    def sends(number):
        sx, sy = SIDES[number]
        return inside(sx, 0) & inside(0, -sy) if number in corners else inside(sx, sy)

    early = column_sides
    late = column_sides + row_sides + corners

    def start_samples(numbers, is_late):
        for number in numbers:

            @pl.when(inside(*SIDES[number]))
            def _():
                sample_copy(number, is_late).start()

    def start_halo(which, numbers):
        for number in numbers:

            @pl.when(sends(number))
            def _():
                for level in which:
                    halo_copy(level, number).start()

    def wait_halo(which, numbers):
        for number in numbers:
            sx, sy = SIDES[number]

            @pl.when(inside(-sx, -sy))
            def _():
                for level in which:
                    halo_copy(level, number).wait_recv()

    fetch["codes"].wait()
    fetch["counts"].wait()
    slots = codes.shape[-1]
    turned_counts[0 : listed_counts.shape[0], 0:patch] = listed_counts[...].astype(F32)
    turned_counts[...] = jnp.transpose(turned_counts[...])
    codes_flat[...] = jnp.full(codes_flat.shape, -1.0, F32)
    slot_lane = lax.broadcasted_iota(jnp.int32, (patch // 2, slots), 1).astype(F32)
    starts = [0]
    for level in range(levels):
        starts.append(starts[-1] + (patch >> (level + 1)) ** 2)
    for level in range(levels):
        size = patch >> level
        half = size // 2
        for row in range(size):
            for bit in range(2):
                begin = ((row << level) * patch + (bit << level)) * levels + level
                if half > 1:
                    listed = codes[pl.ds(begin, half, stride=levels << (level + 1)), :]
                    column = pl.ds(bit << level, half, stride=2 << level)
                else:
                    listed = codes[pl.ds(begin, 1), :]
                    column = pl.ds(bit << level, 1)
                lane = (row << level) * levels + level
                count = turned_counts[column, :][:, lane : lane + 1]
                spot = starts[level] + (row // 2) * half
                codes_flat[row % 2 * 2 + bit, spot : spot + half, 0:slots] = jnp.where(
                    slot_lane[:half] < count, listed.astype(F32), -1.0
                )
    fetch["upper"].wait()
    turns = [jnp.transpose(codes_flat[parity])[0:slots] for parity in range(4)]
    begin = 0
    upper_codes = codes_upper[...].astype(F32)
    upper_lane = lax.broadcasted_iota(jnp.int32, upper_codes.shape, 1)
    slot_row = lax.broadcasted_iota(jnp.int32, (slots, 1), 0)
    group_lane = lax.broadcasted_iota(jnp.int32, (slots, GROUP), 1)
    for step in range(steps):
        cols = along >> step
        index = begin + (row_index // 2**step) * cols + col_index // 2**step
        listed = jnp.sum(jnp.where(upper_lane == index, upper_codes, 0.0), axis=1, keepdims=True)
        listed = jnp.where(slot_row < counts_upper[index], listed, -1.0)
        turns[0] = jnp.where(group_lane == KEPT - 8 + step, listed, turns[0])
        begin += (across >> step) * cols
    for parity in range(4):
        turned[0:slots, parity * GROUP : (parity + 1) * GROUP] = turns[parity]
    code = lax.broadcasted_iota(jnp.int32, (CODE_ROWS, GROUP), 0).astype(F32)
    founds = []
    for parity in range(4):
        found = jnp.zeros((GROUP, GROUP), F32)[0:CODE_ROWS]
        for slot in range(slots):
            listed = turned[slot : slot + 1, parity * GROUP : (parity + 1) * GROUP]
            found = jnp.where(code == listed, 1.0, found)
        found = jnp.concatenate([found, jnp.zeros((GROUP - CODE_ROWS, GROUP), F32)], axis=0)
        founds.append(jnp.transpose(found)[0:KEPT, 0:CODE_ROWS].astype(BF16))
    fetch["table"].wait()
    fetch["table_upper"].wait()
    for parity in range(4):
        masks[parity] = dot(founds[parity], table[parity], NN)
    upper_masks[...] = dot(founds[0][KEPT - 16 :], table_upper[...], NN)[8:]

    pl.semaphore_wait(barrier, len(moves))

    fetch["basis"].wait()
    own_basis = twice(basis[...])

    def project(number, carry):
        rows_in(number).wait()
        rows = samples[pl.ds(1 + number * chunk, chunk), 1 : 1 + patch].reshape(-1, sources)
        wide = dot(rows, own_basis, NT).reshape(chunk, patch * vectors, lanes)
        for row in range(chunk):
            padded[0][number * chunk + row + 2, 1 : 1 + patch // 2] = pair_columns(
                wide[row], vectors, rank
            )
            if row % 2 == 0:
                swapped[0][number * (chunk // 2) + row // 2, 1 : 1 + patch // 2] = pair_columns(
                    wide[row], vectors, rank, True
                )
        return carry

    lax.fori_loop(0, patch // chunk, project, 0)
    start_halo([0], column_sides + row_sides)
    fetch["transfer"].wait()

    for level in range(levels):
        child = padded[level]
        matrix = twice(transfer[level])
        cols = patch >> (level + 1)
        grouped = jnp.concatenate(
            [
                jnp.concatenate(
                    [child[2 * row + 2, 1 : 1 + cols], child[2 * row + 3, 1 : 1 + cols]], axis=-1
                ).reshape(-1, 4 * rank)
                for row in range(cols)
            ],
            axis=0,
        )
        lifted = dot(grouped, matrix, NT)
        if level < levels - 1:
            lifted = lifted.reshape(cols, cols * vectors, lanes)
            for row in range(cols):
                padded[level + 1][row + 2, 1 : 1 + cols // 2] = pair_columns(
                    lifted[row], vectors, rank
                )
                if row % 2 == 0:
                    swapped[level + 1][row // 2, 1 : 1 + cols // 2] = pair_columns(
                        lifted[row], vectors, rank, True
                    )
        else:
            half = vectors // 2
            tops[row_index, col_index] = jnp.where(
                low_half((half, lanes), rank), lifted[:half], lifted[half:]
            ).astype(BF16)

    start_halo(range(levels - 1, 0, -1), column_sides + row_sides)
    for dr, dc in moves:
        top_copy(dr, dc).start()

    fetch["coupling"].wait()

    def shift(level, carry):
        for part in range(coupling.shape[2]):
            coupling[0, level, part, :, 0 : 6 * rank] = coupling[1, level, part, :, rank : 7 * rank]
        return carry

    lax.fori_loop(0, coupling.shape[1], shift, 0)
    low_lanes = low_half((1, lanes), rank).astype(F32).astype(BF16)
    high_lanes = 1 - low_lanes

    def weights(level, row_bit):
        sides = []
        for col_bit in range(2):
            parts = []
            for kind, row, pair, other, _, _ in PAIRS[row_bit, col_bit]:
                spot = pl.ds(pair * lanes, lanes)
                part = coupling[col_bit, level, row + 1 - row_bit, :, spot]
                if kind == "both":
                    second = coupling[1 - col_bit, level, other + 1 - row_bit, :, spot]
                    if col_bit == 0:
                        part = part * low_lanes + second * high_lanes
                    else:
                        part = part * high_lanes + second * low_lanes
                parts.append(part)
            parts = jnp.concatenate(parts, axis=-1)
            blank = jnp.zeros_like(parts)
            sides.append(jnp.concatenate([parts, blank] if col_bit == 0 else [blank, parts], axis=0))
        return jnp.concatenate(sides, axis=-1)

    def couple(level, cells):
        cols = patch >> (level + 1)
        for row_bit in range(2):
            left = []
            for row, col in cells:
                line = []
                for col_bit in range(2):
                    spot = starts[level] + row * cols + col
                    mask = masks[row_bit * 2 + col_bit, pl.ds(spot, 1), :]
                    mask = jnp.broadcast_to(mask, (16, PAIR_COUNT * lanes)).astype(BF16)
                    parts = []
                    for kind, part_row, pair, _, _, _ in PAIRS[row_bit, col_bit]:
                        part = padded[level][2 * row + part_row, col + pair]
                        if kind == "both":
                            second = swapped[level][row, col + pair]
                            if col_bit == 0:
                                part = part * low_lanes + second * high_lanes
                            else:
                                part = part * high_lanes + second * low_lanes
                        parts.append(part)
                    parts = jnp.concatenate(parts, axis=-1)
                    parts = parts.reshape(-1, 16, PAIR_COUNT * lanes) * mask[None]
                    line.append(parts.reshape(vectors, PAIR_COUNT * lanes))
                left.append(jnp.concatenate(line, axis=-1))
            image = dot(jnp.concatenate(left, axis=0), weights(level, row_bit), NT)
            image = image.reshape(len(cells), vectors, lanes)
            for number, (row, col) in enumerate(cells):
                images[level][2 * row + row_bit, col] = image[number]

    inner = range(1, patch // 2 - 1)

    def inner_rows(pair, carry):
        couple(0, [(1 + 2 * pair + step, col) for step in range(2) for col in inner])
        return carry

    lax.fori_loop(0, len(inner) // 2, inner_rows, 0)

    last = patch // 2 - 1
    own = range(levels)
    wait_halo([0], row_sides)
    couple(0, [(row, col) for row in (0, last) for col in inner])
    fetch["near"].wait()
    strip = 2

    def near_body(number, carry):
        spot = pl.ds(number * strip, strip)
        left = jnp.concatenate(
            [
                samples[pl.ds(number * strip + row, strip), col : col + patch].reshape(-1, sources)
                for row in range(3)
                for col in range(3)
            ],
            axis=-1,
        )
        flat = jnp.concatenate([near[tile] for tile in range(9)], axis=-1)
        near_sum[spot] = dot(left, flat, NT).reshape(strip, patch * vectors, sources)
        return carry

    start_samples(early, 0)
    start_samples(late, 1)
    lax.fori_loop(0, patch // strip - 2, near_body, 0, unroll=2)
    wait_halo(own, column_sides)
    start_halo(own, corners)
    lax.fori_loop(patch // strip - 2, patch // strip, near_body, 0, unroll=2)
    for level in range(levels):
        rows, cols = patch >> (level + 1), (patch >> (level + 1)) + 2
        for edge in (0, cols - 1):
            for row in range(rows):
                piece = padded[level][2 * row + 2, edge].astype(F32)
                swapped[level][row, edge] = pltpu.roll(piece, rank, 1).astype(BF16)

    wait_halo(range(1, levels), row_sides)
    wait_halo(own, corners)
    couple(0, [(row, col) for row in range(patch // 2) for col in (0, last)])
    for dr, dc in moves:
        top_copy(dr, dc, (row_index - dr) % across, (col_index - dc) % along).wait_recv()
    for is_late, numbers in enumerate((early, late)):
        for number in numbers:

            @pl.when(inside(-SIDES[number][0], -SIDES[number][1]))
            def _():
                sample_copy(number, is_late).wait_recv()

    def window(ref, row, col):
        return jnp.concatenate(
            [ref[row + code, col + step] for code in range(6) for step in range(3)], axis=-1
        )

    uppers[0][...] = jnp.zeros(uppers[0].shape, BF16)
    for row in range(across):
        for col in range(along // 2):
            even, odd = (tops[row, 2 * col + bit].astype(F32) for bit in range(2))
            low = low_half(even.shape, rank)
            first = jnp.where(low, even, pltpu.roll(odd, rank, 1))
            second = jnp.where(low, pltpu.roll(even, rank, 1), odd)
            both = jnp.concatenate([first, second], axis=0)
            uppers[0][row + 2, col + 1] = both.astype(BF16)
    top_matrix = twice(transfer[levels])
    for step in range(steps - 1):
        child, parent = uppers[step], uppers[step + 1]
        parent[...] = jnp.zeros(parent.shape, BF16)
        rows, cols = across >> step, along >> (step + 1)
        grouped = jnp.concatenate(
            [
                jnp.concatenate(
                    [child[2 * row + 2, 1 : 1 + cols], child[2 * row + 3, 1 : 1 + cols]], axis=-1
                ).reshape(-1, 4 * rank)
                for row in range(rows // 2)
            ],
            axis=0,
        )
        lifted = dot(grouped, top_matrix, NT).reshape(rows // 2, cols * vectors, lanes)
        for row in range(rows // 2):
            parent[row + 2, 1 : 1 + cols // 2] = pair_columns(lifted[row], vectors, rank)
    low = low_half((vectors, lanes), rank)
    upper_images = []
    for step in range(steps):
        row, col = row_index // 2**step, col_index // 2**step
        slab = window(uppers[step], 2 * (row // 2), col // 2)
        mask = jnp.broadcast_to(upper_masks[step : step + 1, :], (16, 36 * rank)).astype(BF16)
        slab = (slab.reshape(-1, 16, 36 * rank) * mask[None]).reshape(slab.shape)
        flat = jnp.concatenate(
            [coupling[col % 2, levels, code + 1 - row % 2, :, 0 : 6 * rank] for code in range(6)],
            axis=-1,
        )
        upper_images.append(dot(slab, twice(flat), NT))
    for level in range(1, levels):
        size = patch >> (level + 1)
        couple(level, [(row, col) for row in range(size) for col in range(size)])
    down = upper_images[-1]
    for step in range(steps - 2, -1, -1):
        row, col = row_index // 2**step, col_index // 2**step
        carried = dot(down.astype(BF16) * low_lanes, top_matrix, NN)
        part = jnp.where(row % 2 == 0, carried[:, :lanes], carried[:, lanes:])
        part = jnp.where(low == (col % 2 == 0), part, pltpu.roll(part, rank, 1))
        down = upper_images[step] + part

    for level in range(levels - 1, -1, -1):
        size = patch >> (level + 1)
        if level == levels - 1:
            parent = down.astype(BF16) * low_lanes
        else:
            parent = jnp.concatenate(
                [split_columns(downs[level + 1][row], rank) for row in range(size)], axis=0
            )
        carried = dot(parent, twice(transfer[level]), NN)
        carried = carried.reshape(size, size, vectors, 2 * lanes)
        for row in range(size):
            for row_bit in range(2):
                spot = 2 * row + row_bit
                part = carried[row, :, :, row_bit * lanes : (row_bit + 1) * lanes]
                downs[level][spot] = (images[level][spot] + part).astype(BF16)

    for side, column, step in ((0, 0, 0), (1, patch - 1, 2)):
        left = jnp.concatenate(
            [col_rims[side, part : part + patch, 0].reshape(-1, sources) for part in range(3)],
            axis=-1,
        )
        flat = jnp.concatenate([near[3 * part + step] for part in range(3)], axis=-1)
        spot = pl.ds(column * vectors, vectors)
        extra = dot(left, flat, NT).reshape(patch, vectors, sources)
        near_sum[:, spot, :] = near_sum[:, spot, :] + extra
    for side, row, step in ((0, 0, 0), (1, patch - 1, 6)):
        left = jnp.concatenate(
            [row_rims[side, part : part + patch].reshape(-1, sources) for part in range(3)],
            axis=-1,
        )
        flat = jnp.concatenate([near[step + part] for part in range(3)], axis=-1)
        near_sum[row] = near_sum[row] + dot(left, flat, NT)

    for is_late, numbers in enumerate((early, late)):
        for number in numbers:

            @pl.when(inside(*SIDES[number]))
            def _():
                sample_copy(number, is_late).wait_send()

    for number in range(len(SIDES)):

        @pl.when(sends(number))
        def _():
            for level in range(levels):
                halo_copy(level, number).wait_send()

    for dr, dc in moves:
        top_copy(dr, dc).wait_send()


def finish_kernel(rank, near_sum, down, basis, out_hbm, out, sems):
    patch, _, vectors, sources = out.shape
    chunks = sems.shape[0]
    rows = patch // chunks
    basis2 = twice(basis[...])

    def rows_out(number):
        spot = pl.ds(number * rows, rows)
        return pltpu.make_async_copy(out.at[spot], out_hbm.at[spot], sems.at[number])

    def body(number, carry):
        spot = pl.ds(number * rows, rows)
        far = split_columns(down[spot].reshape(-1, vectors, 2 * rank), rank)
        summed = near_sum[spot].reshape(-1, sources) + dot(far, basis2, NN)
        out[spot] = summed.astype(BF16).reshape(rows, patch, vectors, sources)
        rows_out(number).start()
        return carry

    lax.fori_loop(0, chunks, body, 0)

    def end(number, carry):
        rows_out(number).wait()
        return carry

    lax.fori_loop(0, chunks, end, 0)


def shards(
    samples,
    leaf_basis,
    transfer,
    coupling,
    near_tiles,
    codes_local,
    counts_local,
    codes_upper,
    counts_upper,
):
    patch, _, vectors, sources = samples.shape
    rank = leaf_basis.shape[0]
    levels = transfer.shape[0] - 1
    lanes = 2 * rank
    across, along = lax.axis_size("gx"), lax.axis_size("gy")
    steps = 1
    while across >> steps >= 2:
        steps += 1
    hbm = pl.BlockSpec(memory_space=pltpu.MemorySpace.HBM)
    vmem = pl.BlockSpec(memory_space=pltpu.VMEM)
    slots = codes_local.shape[-1]
    codes = codes_local.reshape(-1, slots)
    listed_counts = counts_local.transpose(0, 2, 1).reshape(-1, patch)
    far_table, upper_table = spread_tables(rank)

    shapes = [(patch >> level, patch >> (level + 1), vectors, lanes) for level in range(levels)]
    near_sum, down, basis = pl.pallas_call(
        functools.partial(main_kernel, levels, rank, steps, (across, along)),
        out_shape=[
            pltpu.VMEM((patch, patch * vectors, sources), F32),
            pltpu.VMEM(shapes[0], BF16),
            pltpu.VMEM(leaf_basis.shape, BF16),
        ],
        in_specs=[hbm] * 4 + [pl.BlockSpec(memory_space=pltpu.SMEM)] + [hbm] * 6,
        out_specs=[vmem] * 3,
        scratch_shapes=[
            pltpu.VMEM((patch + 2, patch + 2, vectors, sources), BF16),
            pltpu.VMEM(codes.shape, jnp.int32),
            pltpu.VMEM(listed_counts.shape, jnp.int32),
            pltpu.VMEM(codes_upper.shape[::-1], jnp.int32),
            pltpu.VMEM((2, patch + 2, vectors, sources), BF16),
            pltpu.VMEM(transfer.shape, BF16),
            pltpu.VMEM((2, *coupling.shape), BF16),
            pltpu.VMEM(near_tiles.shape, BF16),
            pltpu.VMEM(far_table.shape, BF16),
            pltpu.VMEM(upper_table.shape, BF16),
            pltpu.SemaphoreType.DMA((9 + patch // 4,)),
            pltpu.VMEM((4, GROUP, GROUP), F32),
            pltpu.VMEM((GROUP, GROUP), F32),
            pltpu.VMEM((32, 4 * GROUP), F32),
            pltpu.VMEM((4, KEPT, PAIR_COUNT * lanes), F32),
            pltpu.VMEM((8, 36 * rank), F32),
            pltpu.VMEM((across, along, vectors // 2, lanes), BF16),
            pltpu.VMEM((2, patch + 2, 1, vectors, sources), BF16),
            pltpu.SemaphoreType.DMA((levels + 2, len(SIDES))),
            pltpu.SemaphoreType.DMA((levels + 2, len(SIDES))),
            pltpu.SemaphoreType.DMA((across * along,)),
            pltpu.SemaphoreType.DMA((across * along,)),
        ]
        + [pltpu.VMEM((rows + 4, cols + 2, vectors, lanes), BF16) for rows, cols, _, _ in shapes]
        + [pltpu.VMEM((rows // 2, cols + 2, vectors, lanes), BF16) for rows, cols, _, _ in shapes]
        + [pltpu.VMEM(shape, F32) for shape in shapes]
        + [
            pltpu.VMEM(((across >> step) + 4, (along >> (step + 1)) + 2, vectors, lanes), BF16)
            for step in range(steps)
        ]
        + [pltpu.VMEM(shape, BF16) for shape in shapes[1:]],
        compiler_params=pltpu.CompilerParams(
            collective_id=0, has_side_effects=True, vmem_limit_bytes=VMEM_LIMIT
        ),
        name="main",
    )(
        samples,
        codes,
        listed_counts,
        codes_upper.T,
        counts_upper,
        leaf_basis,
        transfer,
        coupling,
        near_tiles,
        jnp.asarray(far_table),
        jnp.asarray(upper_table),
    )
    return pl.pallas_call(
        functools.partial(finish_kernel, rank),
        out_shape=jax.ShapeDtypeStruct(samples.shape, BF16),
        in_specs=[vmem] * 3,
        out_specs=hbm,
        scratch_shapes=[
            pltpu.VMEM(samples.shape, BF16),
            pltpu.SemaphoreType.DMA((patch // 4,)),
        ],
        compiler_params=pltpu.CompilerParams(vmem_limit_bytes=FINISH_LIMIT),
        name="finish",
    )(near_sum, down, basis)


def solution(mesh):
    placed = (
        P("gx", "gy", None, None),
        P(),
        P(),
        P(),
        P(),
        P("gx", "gy", None, None),
        P("gx", "gy", None),
        P(),
        P(),
    )
    return jax.shard_map(
        shards, mesh=mesh, in_specs=placed, out_specs=P("gx", "gy", None, None), check_vma=False
    )
```
